512 devices in a mesh: dp: 8 (over x, core), ctx: 64 (over y, z).
Axes of the slice: x: 4, y: 8, z: 8, core: 2. Of those that a mesh axis runs over, the one named last changes fastest.
Arguments:
- queries: bfloat16 [8192, 4096], P(('dp', 'ctx')), may hold values from -150 to 150
- keys: bfloat16 [131072, 1024], P(('dp', 'ctx')), may hold values from -8 to 8
- values: bfloat16 [131072, 1024], P(('dp', 'ctx')), may hold values from -6 to 6
- learned_compress_queries: bfloat16 [16, 1024], replicated, may hold values from -150 to 150
- span_len: int32 [8, 64], P('dp', 'ctx'), may hold values from 1 to 16, 768 in all within a row
- span_offset: int32 [8, 64], P('dp', 'ctx'), may hold values from 0 to 240
- destination: int32 [8192, 1], P(('dp', 'ctx')), may hold values from 0 to 63; in each aligned block of 16 rows (0 to 15, 16 to 31, ...) at most 2 rows name the same one
- cotangent: bfloat16 [8192, 4096], P(('dp', 'ctx')), may hold values from -6 to 6
- adapter_a: bfloat16 [64, 16, 4096], P('ctx'), may hold values from -0.09375 to 0.09375
- adapter_b: bfloat16 [64, 16, 4096], P('ctx'), may hold values from -0.09375 to 0.09375
Outputs:
- grad_rows: bfloat16 [8192, 4096], P(('dp', 'ctx'))
- grad_a: float32 [64, 16, 4096], P('ctx')
- grad_b: float32 [64, 16, 4096], P('ctx')
The draws below stay inside these ranges and needn't reach their ends.
Inputs may be any that keep to these rules, and one draw needn't show every extreme that they name: `destination`: in each device's 16 slots (aligned blocks of rows) no decoder is named more than 2 times, a bound that some block reaches.
All inputs are finite; a program needn't handle non-finite values. No bound on the sum of `span_len` on one device may be relied on, other than what follows from the above.
Results may differ from the reference program's by a relative error of at most 0.025.
Values may be sent and summed in bfloat16 or wider, within the bound.
A program may use at most 64 MiB of HBM per device.

```python
import math
import jax
import jax.numpy as jnp
import numpy as np
from jax import lax

MODEL_WIDTH = 4096
QUERY_HEADS = 32
KEY_VALUE_HEADS = 8
HEAD_SIZE = 128
COMPRESSED_ROWS = 16
R = 16
SEGMENT_TOKENS = 256
SPAN_SLOT_LIMIT = 16
CAP = 2
ALL_TOKENS = 131072
ROWS = 8192
N_DP = 8
N_CTX = 64


def key_rows(key):
    random_base_key = jax.random.fold_in(key, 11)
    row_block = jax.random.truncated_normal(random_base_key, -6.0, 6.0, (ALL_TOKENS, KEY_VALUE_HEADS * HEAD_SIZE), jnp.float32)
    return row_block


def draw_keys(key, part):
    return key_rows(key).astype(jnp.bfloat16)


def draw_queries(key, part):
    random_base_key = jax.random.fold_in(key, 21)
    base_offset = jax.random.truncated_normal(random_base_key, -6.0, 6.0, (ROWS, MODEL_WIDTH), jnp.float32)
    return base_offset.astype(jnp.bfloat16)


def draw_learned_compress_queries(key, part):
    random_base_key = jax.random.fold_in(key, 31)
    base_offset = 3.0 * jax.random.truncated_normal(random_base_key, -5.0, 5.0, (COMPRESSED_ROWS, KEY_VALUE_HEADS * HEAD_SIZE), jnp.float32)
    return base_offset.astype(jnp.bfloat16)


def set_ends(entries, own_key, least, largest):
    dims = entries.shape
    spot = [jax.random.randint(jax.random.fold_in(own_key, axis), (), 0, dims[axis]) for axis in range(len(dims))]
    entries = entries.at[tuple(spot)].set(least)
    longest = dims.index(max(dims))
    spot[longest] = (spot[longest] + 1) % dims[longest]
    return entries.at[tuple(spot)].set(largest)


def steps_of(stream_key, dims, shards, least, top_value):
    gain = 1.0
    for dim, blocks in shards:
        steps = jax.random.uniform(jax.random.fold_in(jax.random.fold_in(stream_key, 6), dim), (blocks,), jnp.float32, least / len(shards), top_value / len(shards))
        gain = gain * jnp.repeat(jnp.exp(steps), dims[dim] // blocks).reshape((-1,) + (1,) * (len(dims) - 1 - dim))
    return gain


def length_profile(number_of, total, limit, skew):
    weights = [(1 << 20) // math.isqrt(rank ** skew) + 1 for rank in range(2, number_of + 1)]
    surplus, holding = total - limit - (number_of - 1), [1] * (number_of - 1)
    while surplus > 0:
        candidates = [i for i in range(number_of - 1) if holding[i] < limit]
        whole, left = sum([weights[i] for i in candidates]), surplus
        for i in candidates:
            addition = min(limit - holding[i], max(1, left * weights[i] // whole), surplus)
            holding[i] = holding[i] + addition
            surplus = surplus - addition
    return np.array([limit] + holding)


def ragged_sizes(own_key, amount, total, reach, lean):
    if amount == 2:
        one = jax.random.randint(own_key, (), max(1, total - reach), min(reach, total - 1) + 1)
        return jnp.stack([one, total - one])
    sizes = jnp.asarray(length_profile(amount, total, reach, lean), jnp.int32)
    pairs = (amount - 1) // 2
    donor, taker = sizes[1:1 + 2 * pairs:2], sizes[2:2 + 2 * pairs:2]
    margin = jnp.minimum(donor - 1, reach - taker)
    moved = jax.random.randint(jax.random.fold_in(own_key, 1), (pairs,), 0, 1 << 20) % (margin + 1)
    sizes = sizes.at[1:1 + 2 * pairs:2].set(donor - moved).at[2:2 + 2 * pairs:2].set(taker + moved)
    return sizes[jax.random.permutation(jax.random.fold_in(own_key, 2), amount)]


def routed_block(rng, own, number, rows, number_of, top, limit, slope):
    order = jax.random.permutation(rng, number_of)
    heavy_load, usual = portions_of(number_of, rows * top, limit, slope, True), portions_of(number_of, rows * top, limit, slope, False)
    places = jnp.arange(number_of)

    def named(sizes, rotation):
        used = int((sizes > 0).sum())
        fixed = max(1, used // 4)
        passed = fixed + (places - fixed + rotation * (used - fixed)) % max(1, number_of - fixed)
        return jnp.zeros((number_of,), jnp.int32).at[order[jnp.where(places < fixed, places, passed)]].set(jnp.asarray(sizes, jnp.int32))

    sizes = jnp.where(number % 4 == 0, named(heavy_load, number // 4), named(usual, number - number // 4 - 1))
    mixed = jax.random.permutation(jax.random.fold_in(own, 3), number_of)
    giver, receiver = mixed[0:number_of // 2 * 2:2], mixed[1:number_of // 2 * 2:2]
    room = jnp.minimum(sizes[giver] - 1, limit - sizes[receiver]) // 2
    room = jnp.where((giver == order[0]) | (receiver == order[0]) | (sizes[receiver] == 0), 0, jnp.maximum(room, 0))
    passed = jax.random.randint(jax.random.fold_in(own, 4), (number_of // 2,), 0, 1 << 20) % (room + 1)
    sizes = sizes.at[giver].add(-passed).at[receiver].add(passed)
    members = jnp.searchsorted(jnp.cumsum(sizes), jnp.arange(rows * top), side="right").astype(jnp.int32)
    table = members.reshape(top, rows).T
    table = table[jax.random.permutation(jax.random.fold_in(own, 1), rows)]
    rotation = jax.random.randint(jax.random.fold_in(own, 2), (rows, 1), 0, top)
    return jnp.take_along_axis(table, (jnp.arange(top)[None, :] + rotation) % top, axis=1)


def portions_of(amount, total, limit, lean, full):
    loads = [(1 << 20) // math.isqrt(standing ** lean) + 1 for standing in range(1, amount + 1)]
    largest = limit if full else min(limit, max(-(-total // amount), total * loads[0] // sum(loads)))
    least = 1 if total - largest >= amount - 1 else 0
    holding, spare = [largest] + [least] * (amount - 1), total - largest - least * (amount - 1)
    while spare > 0:
        movable = [i for i in range(1, amount) if holding[i] < largest] or [i for i in range(1, amount) if holding[i] < limit]
        mass, remaining = sum([loads[i] for i in movable]), spare
        for i in movable:
            more = min(limit - holding[i], max(1, remaining * loads[i] // mass), spare)
            holding[i] = holding[i] + more
            spare = spare - more
    return np.array(holding)


def bell_draw(stream_key, dims, scale, limit, cuts=(), held_as=jnp.bfloat16):
    gain = steps_of(stream_key, dims, cuts, -0.22, 0.18) if cuts else 1.0
    entries = jax.random.normal(stream_key, dims, jnp.float32) * scale * gain
    return jnp.minimum(jnp.maximum(entries, -limit), limit).astype(held_as)


def setup_inputs(seed: int = 0) -> dict:
    arg_keys = jax.random.split(jax.random.key(seed), 11)
    queries = draw_queries(jax.random.fold_in(arg_keys[10], 71), 0)
    keys = draw_keys(jax.random.fold_in(arg_keys[10], 71), 0)
    values = bell_draw(arg_keys[2], (ALL_TOKENS, KEY_VALUE_HEADS * HEAD_SIZE), 1.0, 6.0, ((0, 512),))
    learned_compress_queries = draw_learned_compress_queries(jax.random.fold_in(arg_keys[10], 71), 0)
    span_len = jax.vmap(lambda own: ragged_sizes(own, N_CTX, 3 * N_CTX * SPAN_SLOT_LIMIT // 4, SPAN_SLOT_LIMIT, 2))(jax.random.split(arg_keys[4], N_DP)).reshape((N_DP, N_CTX)).astype(jnp.int32)
    span_offset = set_ends(jax.random.randint(arg_keys[5], (N_DP, N_CTX), 0, SEGMENT_TOKENS - SPAN_SLOT_LIMIT + 1), jax.random.fold_in(arg_keys[5], 1), 0, SEGMENT_TOKENS - SPAN_SLOT_LIMIT).astype(jnp.int32)
    destination_keys = jax.random.split(jax.random.fold_in(arg_keys[6], 1), ROWS // SPAN_SLOT_LIMIT)
    destination_turns = jax.random.permutation(jax.random.fold_in(arg_keys[6], 3), ROWS // SPAN_SLOT_LIMIT)
    destination = jax.vmap(lambda own, number: routed_block(jax.random.fold_in(arg_keys[6], 2), own, number, SPAN_SLOT_LIMIT, N_CTX, 1, CAP, 2))(destination_keys, destination_turns).reshape((ROWS, 1))
    cotangent = bell_draw(arg_keys[7], (ROWS, MODEL_WIDTH), 1.0, 6.0, ((0, 512),))
    adapter_a = bell_draw(arg_keys[8], (N_CTX, R, MODEL_WIDTH), MODEL_WIDTH ** -0.5, 0.09375, ((0, 64),))
    adapter_b = bell_draw(arg_keys[9], (N_CTX, R, MODEL_WIDTH), MODEL_WIDTH ** -0.5, 0.09375, ((0, 64),))
    return {"queries": queries, "keys": keys, "values": values, "learned_compress_queries": learned_compress_queries, "span_len": span_len, "span_offset": span_offset, "destination": destination, "cotangent": cotangent, "adapter_a": adapter_a, "adapter_b": adapter_b}


SCALE = 2.0
EPS = 1e-06

def reference(queries, keys, values, learned_compress_queries, span_len, span_offset, destination, cotangent, adapter_a, adapter_b):
    query_group = QUERY_HEADS // KEY_VALUE_HEADS
    segment_stack = N_DP * N_CTX
    score_matrix = 1.0 / math.sqrt(HEAD_SIZE)
    segment_keys = keys.reshape(segment_stack, SEGMENT_TOKENS, KEY_VALUE_HEADS, HEAD_SIZE)
    segment_values = values.reshape(segment_stack, SEGMENT_TOKENS, KEY_VALUE_HEADS, HEAD_SIZE)
    compressor_query = learned_compress_queries.astype(jnp.float32).reshape(COMPRESSED_ROWS, KEY_VALUE_HEADS, HEAD_SIZE)

    def compress(item):
        expanded_keys, expanded_values = item
        flat_keys = expanded_keys.astype(jnp.float32)
        flat_values = expanded_values.astype(jnp.float32)
        attention_score = jnp.einsum('cpf,ipf->pci', compressor_query, flat_keys) * score_matrix
        softmax_weight = jax.nn.softmax(attention_score, axis=-1).astype(jnp.bfloat16).astype(jnp.float32)
        compressed_keys = jnp.einsum('wio,owx->iwx', softmax_weight, flat_keys).astype(jnp.bfloat16)
        compressed_values = jnp.einsum('wio,owx->iwx', softmax_weight, flat_values).astype(jnp.bfloat16)
        return (compressed_keys, compressed_values)
    compressed_keys, compressed_values = lax.map(compress, (segment_keys, segment_values))
    compressed_keys = compressed_keys.reshape(N_DP, N_CTX * COMPRESSED_ROWS, KEY_VALUE_HEADS, HEAD_SIZE)
    compressed_values = compressed_values.reshape(N_DP, N_CTX * COMPRESSED_ROWS, KEY_VALUE_HEADS, HEAD_SIZE)
    segment_queries = queries.reshape(segment_stack, SPAN_SLOT_LIMIT, KEY_VALUE_HEADS, query_group, HEAD_SIZE)
    offs = span_offset.reshape(segment_stack)
    lens = span_len.reshape(segment_stack)
    dyseg = cotangent.reshape(segment_stack, SPAN_SLOT_LIMIT, MODEL_WIDTH)

    def attend(item):
        query_matrix, expanded_keys, expanded_values, off, size, dyrows, index = item
        doc = index // N_CTX
        seg_pos = index % N_CTX
        kall = jnp.concatenate([expanded_keys, compressed_keys[doc]], axis=0).astype(jnp.float32)
        vall = jnp.concatenate([expanded_values, compressed_values[doc]], axis=0).astype(jnp.float32)
        pos = off + jnp.arange(SPAN_SLOT_LIMIT, dtype=jnp.int32)
        local = jnp.arange(SEGMENT_TOKENS, dtype=jnp.int32)[None, :] <= pos[:, None]
        source = jnp.arange(N_CTX * COMPRESSED_ROWS, dtype=jnp.int32) // COMPRESSED_ROWS
        far = jnp.broadcast_to((source < seg_pos)[None, :], (SPAN_SLOT_LIMIT, N_CTX * COMPRESSED_ROWS))
        seen = jnp.concatenate([local, far], axis=1)[:, None, None, :]
        attention_score = jnp.einsum('shgd,nhd->shgn', query_matrix.astype(jnp.float32), kall) * score_matrix
        attention_score = jnp.where(seen, attention_score, -jnp.inf)
        peak = lax.optimization_barrier(jnp.max(attention_score, axis=-1, keepdims=True))
        prob = jnp.where(seen, jnp.exp(attention_score - peak), 0.0)
        total = lax.optimization_barrier(jnp.sum(prob, axis=-1))
        pb = prob.astype(jnp.bfloat16).astype(jnp.float32)
        accum = jnp.einsum('shgn,nhd->shgd', pb, vall)
        out = (accum / total[..., None]).reshape(SPAN_SLOT_LIMIT, MODEL_WIDTH)
        live = (jnp.arange(SPAN_SLOT_LIMIT, dtype=jnp.int32) < size)[:, None]
        attn = jnp.where(live, out, 0.0).astype(jnp.bfloat16)
        dy = jnp.where(live, dyrows, jnp.zeros_like(dyrows))
        return (attn, dy)
    attn, dy = lax.map(attend, (segment_queries, segment_keys, segment_values, offs, lens, dyseg, jnp.arange(segment_stack, dtype=jnp.int32)))
    block = 256 if ROWS % 256 == 0 else SPAN_SLOT_LIMIT
    attn = attn.reshape(ROWS // block, block, MODEL_WIDTH)
    dy = dy.reshape(ROWS // block, block, MODEL_WIDTH)
    dest = destination[:, 0].reshape(ROWS // block, block)

    def decode(carry, item):
        grad_a, grad_b = carry
        row_block, dyrows, target = item
        x = row_block.astype(jnp.float32)
        g = dyrows.astype(jnp.float32)
        rs = lax.rsqrt(lax.optimization_barrier(jnp.mean(x * x, axis=-1, keepdims=True)) + EPS)
        nrm = x * rs
        normed = nrm.astype(jnp.bfloat16).astype(jnp.float32)
        amat = adapter_a[target].astype(jnp.float32)
        bmat = adapter_b[target].astype(jnp.float32)
        hid = jnp.einsum('bk,brk->br', normed, amat).astype(jnp.bfloat16).astype(jnp.float32)
        back = (SCALE * jnp.einsum('bk,brk->br', g, bmat)).astype(jnp.bfloat16).astype(jnp.float32)
        term_b = SCALE * (hid[:, :, None] * g[:, None, :])
        term_a = back[:, :, None] * normed[:, None, :]
        grad_b = grad_b + jax.ops.segment_sum(term_b, target, num_segments=N_CTX)
        grad_a = grad_a + jax.ops.segment_sum(term_a, target, num_segments=N_CTX)
        dn = jnp.einsum('br,brk->bk', back, amat)
        grad = g + rs * (dn - nrm * lax.optimization_barrier(jnp.mean(dn * nrm, axis=-1, keepdims=True)))
        return ((grad_a, grad_b), grad.astype(jnp.bfloat16))
    zero_block = jnp.zeros((N_CTX, R, MODEL_WIDTH), jnp.float32)
    (grad_a, grad_b), grad_rows = lax.scan(decode, (zero_block, zero_block), (attn, dy, dest))
    return (grad_rows.reshape(ROWS, MODEL_WIDTH), grad_a, grad_b)
```

```python
import functools
import math

import jax
import jax.numpy as jnp
from jax import lax
from jax.experimental import pallas as pl
from jax.experimental.pallas import tpu as pltpu
from jax.sharding import Mesh
from jax.sharding import PartitionSpec as P

QUERY_HEADS = 32
KEY_VALUE_HEADS = 8
GROUP = QUERY_HEADS // KEY_VALUE_HEADS
HEAD_SIZE = 128
COMPRESSED_ROWS = 16
RANK = 16
SLOTS = 16

SCALE = 2.0
EPS = 1e-06
NEGATIVE_FLOOR = -1e30
SOFTMAX_SCALE = 1.0 / math.sqrt(HEAD_SIZE)
HIGH = lax.Precision.HIGHEST


def routes(kind, sizes, me):
    dp, y, z = me
    ndp, ny, nz = sizes
    if kind == "plane":
        def route(i):
            yy, zz = i // nz, i % nz
            return {"dp": dp, "y": yy, "z": zz}, zz
        return ny * nz, route, y * nz + z
    if kind == "owners":
        def route(i):
            pp, zz = i // nz, i % nz
            return {"dp": pp, "y": dp, "z": zz}, zz
        return ndp * nz, route, y * nz + z
    axis, form = kind.split("_")
    n = {"dp": ndp, "y": ny, "z": nz}[axis]
    own = {"dp": dp, "y": y, "z": z}[axis]

    def route(i):
        where = {"dp": dp, "y": y, "z": z}
        where[axis] = i
        return where, (i if form == "swap" else None)

    return n, route, own


def exchange_kernel(kinds, sizes, *refs):
    n_items = len(kinds)
    ins, outs = refs[:n_items], refs[n_items : 2 * n_items]
    sems = refs[2 * n_items :]
    me = (lax.axis_index("dp"), lax.axis_index("y"), lax.axis_index("z"))
    dp, y, z = me
    ndp, ny, nz = sizes
    barrier = pltpu.get_barrier_semaphore()
    owners = "owners" in kinds

    greeted = []
    if "plane" in kinds:
        greeted.append("plane")
    for axis in ("z", "y", "dp"):
        if any(kind.startswith(axis + "_") for kind in kinds):
            if not (axis in ("y", "z") and "plane" in kinds):
                greeted.append(axis + "_spread")
    expected = 0
    for kind in greeted:
        n, route, own = routes(kind, sizes, me)

        def greet(step, carry, n=n, route=route, own=own):
            device, _ = route(lax.rem(own + step, n))
            pl.semaphore_signal(
                barrier, inc=1, device_id=device, device_id_type=pl.DeviceIdType.MESH
            )
            return carry

        lax.fori_loop(1, n, greet, 0)
        expected += n - 1
    if owners:
        mine = dp == y

        def greet_sender(i, carry):
            yy, zz = i // nz, lax.rem(i, nz)

            @pl.when(jnp.logical_not(mine & (yy == y) & (zz == z)))
            def _():
                pl.semaphore_signal(
                    barrier,
                    inc=1,
                    device_id={"dp": y, "y": yy, "z": zz},
                    device_id_type=pl.DeviceIdType.MESH,
                )

            return carry

        lax.fori_loop(0, ny * nz, greet_sender, 0)
        pl.semaphore_wait(barrier, ndp * nz - mine.astype(jnp.int32))
    if expected:
        pl.semaphore_wait(barrier, expected)

    def remote(item, i):
        kind = kinds[item]
        n, route, own = routes(kind, sizes, me)
        device, block = route(i)
        src = ins[item] if block is None else ins[item].at[block]
        return pltpu.make_async_remote_copy(
            src_ref=src,
            dst_ref=outs[item].at[own],
            send_sem=sems[3 * item].at[i],
            recv_sem=sems[3 * item + 1].at[own],
            device_id=device,
            device_id_type=pl.DeviceIdType.MESH,
        )

    def arrival(item, i):
        kind = kinds[item]
        block = None if kind.endswith("spread") else 0
        src = ins[item] if block is None else ins[item].at[block]
        return pltpu.make_async_remote_copy(
            src_ref=src,
            dst_ref=outs[item].at[i],
            send_sem=sems[3 * item].at[i],
            recv_sem=sems[3 * item + 1].at[i],
            device_id={"dp": dp, "y": y, "z": z},
            device_id_type=pl.DeviceIdType.MESH,
        )

    def local(item):
        kind = kinds[item]
        n, route, own = routes(kind, sizes, me)
        if kind in ("plane", "owners"):
            block = z
        else:
            block = own if kind.endswith("swap") else None
        src = ins[item] if block is None else ins[item].at[block]
        return pltpu.make_async_copy(src, outs[item].at[own], sems[3 * item + 2])

    for item, kind in enumerate(kinds):
        n, route, own = routes(kind, sizes, me)
        if kind == "owners":
            def send(i, carry, item=item):
                self_here = mine & (i == dp * nz + z)

                @pl.when(self_here)
                def _():
                    local(item).start()

                @pl.when(jnp.logical_not(self_here))
                def _():
                    remote(item, i).start()

                return carry

            lax.fori_loop(0, n, send, 0)
        else:
            def send(step, carry, item=item, n=n, own=own):
                remote(item, lax.rem(own + step, n)).start()
                return carry

            lax.fori_loop(1, n, send, 0)
            local(item).start()

    for item, kind in enumerate(kinds):
        n, route, own = routes(kind, sizes, me)
        if kind == "owners":
            def finish(i, carry, item=item):
                @pl.when(jnp.logical_not(mine & (i == dp * nz + z)))
                def _():
                    remote(item, i).wait_send()

                return carry

            lax.fori_loop(0, n, finish, 0)

            def collect(i, carry, item=item):
                @pl.when(jnp.logical_not(mine & (i == y * nz + z)))
                def _():
                    arrival(item, i).wait_recv()

                return carry

            lax.fori_loop(0, ny * nz, collect, 0)

            @pl.when(mine)
            def _(item=item):
                local(item).wait()
        else:
            def finish(step, carry, item=item, n=n, own=own):
                peer = lax.rem(own + step, n)
                remote(item, peer).wait_send()
                arrival(item, peer).wait_recv()
                return carry

            lax.fori_loop(1, n, finish, 0)
            local(item).wait()


def exchange(name, collective_id, sizes, *items):
    arrays = [item[0] for item in items]
    kinds = tuple(item[1] for item in items)
    ndp, ny, nz = sizes
    shapes, scratch = [], []
    for array, kind in zip(arrays, kinds):
        if kind in ("plane", "owners"):
            senders, targets = ny * nz, (ny * nz if kind == "plane" else ndp * nz)
            block = array.shape[1:]
        else:
            senders = targets = {"dp": ndp, "y": ny, "z": nz}[kind.split("_")[0]]
            block = array.shape[1:] if kind.endswith("swap") else array.shape
        shapes.append(jax.ShapeDtypeStruct((senders,) + block, array.dtype))
        scratch += [
            pltpu.SemaphoreType.DMA((targets,)),
            pltpu.SemaphoreType.DMA((senders,)),
            pltpu.SemaphoreType.DMA(()),
        ]
    return pl.pallas_call(
        functools.partial(exchange_kernel, kinds, sizes),
        out_shape=shapes,
        in_specs=[pl.BlockSpec(memory_space=pltpu.VMEM)] * len(arrays),
        out_specs=[pl.BlockSpec(memory_space=pltpu.VMEM)] * len(arrays),
        scratch_shapes=scratch,
        compiler_params=pltpu.CompilerParams(
            collective_id=collective_id, has_side_effects=True
        ),
        name=name,
    )(*arrays)


def compress(keys, values, learned):
    tokens = keys.shape[0]
    k = keys.reshape(tokens, KEY_VALUE_HEADS, HEAD_SIZE)
    v = values.reshape(tokens, KEY_VALUE_HEADS, HEAD_SIZE)
    c = learned.reshape(COMPRESSED_ROWS, KEY_VALUE_HEADS, HEAD_SIZE)
    score = jnp.einsum("cpf,ipf->pci", c, k, preferred_element_type=jnp.float32) * SOFTMAX_SCALE
    weight = jax.nn.softmax(score, axis=-1).astype(jnp.bfloat16)
    short = lambda rows: jnp.einsum(
        "wio,owx->wix", weight, rows, preferred_element_type=jnp.float32
    ).astype(jnp.bfloat16)
    return short(k), short(v)


def attend_local(queries, keys, values, offset):
    slots, tokens = queries.shape[0], keys.shape[0]
    q = queries.reshape(slots, KEY_VALUE_HEADS, GROUP, HEAD_SIZE)
    k = keys.reshape(tokens, KEY_VALUE_HEADS, HEAD_SIZE)
    v = values.reshape(tokens, KEY_VALUE_HEADS, HEAD_SIZE)
    score = jnp.einsum("shgd,nhd->hsgn", q, k, preferred_element_type=jnp.float32) * SOFTMAX_SCALE
    position = offset + jnp.arange(slots, dtype=jnp.int32)
    seen = jnp.arange(tokens, dtype=jnp.int32)[None, :] <= position[:, None]
    seen = seen[None, :, None, :]
    score = jnp.where(seen, score, NEGATIVE_FLOOR)
    peak = jnp.max(score, axis=-1)
    prob = jnp.where(seen, jnp.exp(score - peak[..., None]), 0.0)
    total = jnp.sum(prob, axis=-1)
    acc = jnp.einsum(
        "hsgn,nhd->hsgd", prob.astype(jnp.bfloat16), v, preferred_element_type=jnp.float32
    )
    out = (acc / total[..., None]).astype(jnp.bfloat16)
    return out.reshape(KEY_VALUE_HEADS, slots, GROUP * HEAD_SIZE), peak + jnp.log(total)


def shards(sizes, queries, keys, values, learned, span_len, span_offset, destination, cotangent,
           adapter_a, adapter_b):
    ndp, ny, nz = sizes
    decoders = ny * nz
    model = queries.shape[1]
    wide = model // nz
    narrow = wide // ny
    share = RANK // ndp
    rows = nz * SLOTS
    dp, y = lax.axis_index("dp"), lax.axis_index("y")
    swap = functools.partial(jnp.einsum, "shd->hsd")

    live = (jnp.arange(SLOTS, dtype=jnp.int32) < span_len[0, 0])[:, None]
    dy = jnp.where(live, cotangent, jnp.zeros_like(cotangent))
    ck, cv = compress(keys, values, learned)
    out_local, lse = attend_local(queries, keys, values, span_offset[0, 0])
    by_head = lambda array: array.reshape(SLOTS, nz, wide).transpose(1, 0, 2)
    packet = jnp.concatenate([by_head(queries), by_head(dy), out_local, ck, cv], axis=-1)
    facts = jnp.concatenate([destination.astype(jnp.float32), live.astype(jnp.float32)], axis=1)
    facts = jnp.concatenate([lse, jnp.broadcast_to(facts[None], (nz, SLOTS, 2))], axis=-1)
    facts = jnp.pad(facts, ((0, 0), (0, 0), (0, 128 - facts.shape[-1])))
    part = lambda adapter: lax.dynamic_slice_in_dim(adapter[0], dp * share, share, 0).reshape(
        share, nz, wide
    ).transpose(1, 0, 2)
    adapters = jnp.concatenate([part(adapter_a), part(adapter_b)], axis=1)

    packet, facts, adapters = exchange(
        "heads", 1, sizes, (packet, "z_swap"), (facts, "z_swap"), (adapters, "plane")
    )
    packet = packet.reshape(rows, -1)
    facts = facts.reshape(rows, -1)
    q, dy, out_local = packet[:, :wide], packet[:, wide : 2 * wide], packet[:, 2 * wide : 3 * wide]
    short, adapters = exchange(
        "short", 2, sizes, (packet[:, 3 * wide :], "y_spread"), (adapters, "dp_spread")
    )
    short = short.reshape(ny * rows, 2 * HEAD_SIZE)
    ck, cv = short[:, :HEAD_SIZE], short[:, HEAD_SIZE:]
    lse, target, live = facts[:, :GROUP], facts[:, GROUP : GROUP + 1], facts[:, GROUP + 1 : GROUP + 2]

    heads = q.reshape(rows, GROUP, HEAD_SIZE)
    score = jnp.einsum("rgd,kd->grk", heads, ck, preferred_element_type=jnp.float32) * SOFTMAX_SCALE
    segment = y * nz + jnp.arange(rows, dtype=jnp.int32) // SLOTS
    source = jnp.arange(ny * rows, dtype=jnp.int32) // COMPRESSED_ROWS
    seen = (source[None, :] < segment[:, None])[None]
    score = jnp.where(seen, score, NEGATIVE_FLOOR)
    lse = lse.T
    peak = jnp.maximum(lse, jnp.max(score, axis=-1))
    prob = jnp.where(seen, jnp.exp(score - peak[..., None]), 0.0)
    weight = jnp.exp(lse - peak)
    total = weight + jnp.sum(prob, axis=-1)
    acc = jnp.einsum(
        "grk,kd->grd", prob.astype(jnp.bfloat16), cv, preferred_element_type=jnp.float32
    )
    home = out_local.reshape(rows, GROUP, HEAD_SIZE).transpose(1, 0, 2).astype(jnp.float32)
    attn = (acc + weight[..., None] * home) / total[..., None]
    attn = attn.transpose(1, 0, 2).reshape(rows, wide)
    attn = jnp.where(live > 0.5, attn, 0.0).astype(jnp.bfloat16)

    adapters = adapters.reshape(ndp, decoders, 2, share, wide)
    downs = adapters[:, :, 0].reshape(ndp * decoders * share, wide)
    ups = adapters[:, :, 1].reshape(ndp * decoders * share, wide)
    column = jnp.arange(ndp * decoders * share, dtype=jnp.int32)
    column_decoder = (column // share) % decoders
    column_rank = column // (share * decoders) * share + column % share
    own = target.astype(jnp.int32) == column_decoder[None, :]
    pick = column_rank[:, None] == jnp.arange(RANK, dtype=jnp.int32)[None, :]
    across = (((1,), (1,)), ((), ()))

    def narrowed(left, right):
        full = lax.dot_general(left, right, across, preferred_element_type=jnp.float32)
        return lax.dot_general(
            pick.astype(jnp.float32), jnp.where(own, full, 0.0), (((0,), (1,)), ((), ())),
            precision=HIGH, preferred_element_type=jnp.float32,
        )

    x = attn.astype(jnp.float32)
    square = jnp.sum(x * x, axis=1)[None]
    partial = jnp.concatenate(
        [narrowed(attn, downs), narrowed(dy, ups), square, jnp.zeros((7, rows), jnp.float32)], axis=0
    )
    (partial,) = exchange("sums", 3, sizes, (partial, "z_spread"))
    sums = jnp.sum(partial, axis=0)
    rs = lax.rsqrt(sums[2 * RANK : 2 * RANK + 1] / model + EPS)
    hid_exact = sums[:RANK] * rs
    hid = hid_exact.astype(jnp.bfloat16)
    back = (SCALE * sums[RANK : 2 * RANK]).astype(jnp.bfloat16)
    dot_mean = jnp.sum(back.astype(jnp.float32) * hid_exact, axis=0, keepdims=True) / model
    rs_column, mean_column = rs.T, dot_mean.T
    spread = lax.dot_general(
        back, pick.astype(jnp.bfloat16), (((0,), (1,)), ((), ())), preferred_element_type=jnp.float32
    )
    spread = jnp.where(own, spread, 0.0).astype(jnp.bfloat16)
    dn = jnp.dot(spread, downs, preferred_element_type=jnp.float32)
    nrm = x * rs_column
    d_rows = (dy.astype(jnp.float32) + rs_column * (dn - nrm * mean_column)).astype(jnp.bfloat16)
    normed = nrm.astype(jnp.bfloat16)

    slices = lambda array: array.reshape(rows, ny, narrow).transpose(1, 0, 2)
    columns = jnp.concatenate([slices(normed), slices(dy)], axis=-1)
    small = jnp.concatenate(
        [hid, back, jnp.broadcast_to(target.T, (RANK, rows)).astype(jnp.bfloat16)], axis=0
    )
    d_rows, columns, small = exchange(
        "rows", 4, sizes,
        (d_rows.reshape(nz, SLOTS, wide), "z_swap"), (columns, "y_swap"), (small, "y_spread"),
    )
    grad_rows = d_rows.transpose(1, 0, 2).reshape(SLOTS, model)
    columns = columns.reshape(ny * rows, 2 * narrow)
    small = small.transpose(1, 0, 2).reshape(3 * RANK, ny * rows)
    chosen = (
        small[2 * RANK].astype(jnp.int32)[None, :]
        == jnp.arange(decoders, dtype=jnp.int32)[:, None]
    )[:, None, :]

    def gathered(values_):
        left = jnp.where(chosen, values_[None], jnp.zeros((), jnp.bfloat16))
        return jnp.dot(
            left.reshape(decoders * RANK, ny * rows), columns, preferred_element_type=jnp.float32
        )

    from_hid = SCALE * gathered(small[:RANK])
    from_back = gathered(small[RANK : 2 * RANK])
    is_a = (jnp.arange(2 * narrow, dtype=jnp.int32) < narrow)[None, :]
    terms = jnp.where(is_a, from_back, from_hid).astype(jnp.bfloat16)
    (terms,) = exchange(
        "terms", 5, sizes, (terms.reshape(ny, nz * RANK, 2 * narrow), "dp_swap")
    )
    terms = jnp.sum(terms.astype(jnp.float32), axis=0).astype(jnp.bfloat16)
    (grads,) = exchange("owners", 6, sizes, (terms.reshape(nz, RANK, 2 * narrow), "owners"))
    grads = grads.reshape(ny, nz, RANK, 2, narrow).transpose(3, 2, 1, 0, 4).astype(jnp.float32)
    grads = grads.reshape(2, 1, RANK, model)
    return grad_rows, grads[0], grads[1]


def solution(mesh):
    ndp, nctx = mesh.devices.shape
    nz = KEY_VALUE_HEADS
    sizes = (ndp, nctx // nz, nz)
    fine = Mesh(mesh.devices.reshape(sizes), ("dp", "y", "z"))
    ctx = ("y", "z")
    both = ("dp", "y", "z")
    in_specs = (
        P(both, None),
        P(both, None),
        P(both, None),
        P(),
        P("dp", ctx),
        P("dp", ctx),
        P(both, None),
        P(both, None),
        P(ctx, None, None),
        P(ctx, None, None),
    )
    out_specs = (P(both, None), P(ctx, None, None), P(ctx, None, None))
    return jax.shard_map(
        functools.partial(shards, sizes), mesh=fine, in_specs=in_specs, out_specs=out_specs,
        check_vma=False,
    )
```

```python
import functools
import math

import jax
import jax.numpy as jnp
from jax import lax
from jax.experimental import pallas as pl
from jax.experimental.pallas import tpu as pltpu
from jax.sharding import Mesh
from jax.sharding import PartitionSpec as P

QUERY_HEADS = 32
KEY_VALUE_HEADS = 8
GROUP = QUERY_HEADS // KEY_VALUE_HEADS
HEAD_SIZE = 128
COMPRESSED_ROWS = 16
RANK = 16
SLOTS = 16

SCALE = 2.0
EPS = 1e-06
NEGATIVE_FLOOR = -1e30
SOFTMAX_SCALE = 1.0 / math.sqrt(HEAD_SIZE)
HIGH = lax.Precision.HIGHEST


def routes(kind, sizes, me):
    dp, y, z = me
    ndp, ny, nz = sizes
    if kind == "plane":
        def route(i):
            yy, zz = i // nz, i % nz
            return {"dp": dp, "y": yy, "z": zz}, zz
        return ny * nz, route, y * nz + z
    if kind == "owners":
        def route(i):
            pp, zz = i // nz, i % nz
            return {"dp": pp, "y": dp, "z": zz}, zz
        return ndp * nz, route, y * nz + z
    axis, form = kind.split("_")
    n = {"dp": ndp, "y": ny, "z": nz}[axis]
    own = {"dp": dp, "y": y, "z": z}[axis]

    def route(i):
        where = {"dp": dp, "y": y, "z": z}
        where[axis] = i
        return where, (i if form == "swap" else None)

    return n, route, own


def exchange_kernel(kinds, sizes, *refs):
    n_items = len(kinds)
    ins, outs = refs[:n_items], refs[n_items : 2 * n_items]
    sems = refs[2 * n_items :]
    me = (lax.axis_index("dp"), lax.axis_index("y"), lax.axis_index("z"))
    dp, y, z = me
    ndp, ny, nz = sizes
    barrier = pltpu.get_barrier_semaphore()
    owners = "owners" in kinds

    greeted = []
    if "plane" in kinds:
        greeted.append("plane")
    for axis in ("z", "y", "dp"):
        if any(kind.startswith(axis + "_") for kind in kinds):
            if not (axis in ("y", "z") and "plane" in kinds):
                greeted.append(axis + "_spread")
    expected = 0
    for kind in greeted:
        n, route, own = routes(kind, sizes, me)

        def greet(step, carry, n=n, route=route, own=own):
            device, _ = route(lax.rem(own + step, n))
            pl.semaphore_signal(
                barrier, inc=1, device_id=device, device_id_type=pl.DeviceIdType.MESH
            )
            return carry

        lax.fori_loop(1, n, greet, 0)
        expected += n - 1
    if owners:
        mine = dp == y

        def greet_sender(i, carry):
            yy, zz = i // nz, lax.rem(i, nz)

            @pl.when(jnp.logical_not(mine & (yy == y) & (zz == z)))
            def _():
                pl.semaphore_signal(
                    barrier,
                    inc=1,
                    device_id={"dp": y, "y": yy, "z": zz},
                    device_id_type=pl.DeviceIdType.MESH,
                )

            return carry

        lax.fori_loop(0, ny * nz, greet_sender, 0)
        pl.semaphore_wait(barrier, ndp * nz - mine.astype(jnp.int32))
    if expected:
        pl.semaphore_wait(barrier, expected)

    def remote(item, i):
        kind = kinds[item]
        n, route, own = routes(kind, sizes, me)
        device, block = route(i)
        src = ins[item] if block is None else ins[item].at[block]
        return pltpu.make_async_remote_copy(
            src_ref=src,
            dst_ref=outs[item].at[own],
            send_sem=sems[3 * item].at[i],
            recv_sem=sems[3 * item + 1].at[own],
            device_id=device,
            device_id_type=pl.DeviceIdType.MESH,
        )

    def arrival(item, i):
        kind = kinds[item]
        block = None if kind.endswith("spread") else 0
        src = ins[item] if block is None else ins[item].at[block]
        return pltpu.make_async_remote_copy(
            src_ref=src,
            dst_ref=outs[item].at[i],
            send_sem=sems[3 * item].at[i],
            recv_sem=sems[3 * item + 1].at[i],
            device_id={"dp": dp, "y": y, "z": z},
            device_id_type=pl.DeviceIdType.MESH,
        )

    def local(item):
        kind = kinds[item]
        n, route, own = routes(kind, sizes, me)
        if kind in ("plane", "owners"):
            block = z
        else:
            block = own if kind.endswith("swap") else None
        src = ins[item] if block is None else ins[item].at[block]
        return pltpu.make_async_copy(src, outs[item].at[own], sems[3 * item + 2])

    for item, kind in enumerate(kinds):
        n, route, own = routes(kind, sizes, me)
        if kind == "owners":
            def send(i, carry, item=item):
                self_here = mine & (i == dp * nz + z)

                @pl.when(self_here)
                def _():
                    local(item).start()

                @pl.when(jnp.logical_not(self_here))
                def _():
                    remote(item, i).start()

                return carry

            lax.fori_loop(0, n, send, 0)
        else:
            def send(step, carry, item=item, n=n, own=own):
                remote(item, lax.rem(own + step, n)).start()
                return carry

            lax.fori_loop(1, n, send, 0)
            local(item).start()

    for item, kind in enumerate(kinds):
        n, route, own = routes(kind, sizes, me)
        if kind == "owners":
            def finish(i, carry, item=item):
                @pl.when(jnp.logical_not(mine & (i == dp * nz + z)))
                def _():
                    remote(item, i).wait_send()

                return carry

            lax.fori_loop(0, n, finish, 0)

            def collect(i, carry, item=item):
                @pl.when(jnp.logical_not(mine & (i == y * nz + z)))
                def _():
                    arrival(item, i).wait_recv()

                return carry

            lax.fori_loop(0, ny * nz, collect, 0)

            @pl.when(mine)
            def _(item=item):
                local(item).wait()
        else:
            def finish(step, carry, item=item, n=n, own=own):
                peer = lax.rem(own + step, n)
                remote(item, peer).wait_send()
                arrival(item, peer).wait_recv()
                return carry

            lax.fori_loop(1, n, finish, 0)
            local(item).wait()


def exchange(name, collective_id, sizes, *items):
    arrays = [item[0] for item in items]
    kinds = tuple(item[1] for item in items)
    ndp, ny, nz = sizes
    shapes, scratch = [], []
    for array, kind in zip(arrays, kinds):
        if kind in ("plane", "owners"):
            senders, targets = ny * nz, (ny * nz if kind == "plane" else ndp * nz)
            block = array.shape[1:]
        else:
            senders = targets = {"dp": ndp, "y": ny, "z": nz}[kind.split("_")[0]]
            block = array.shape[1:] if kind.endswith("swap") else array.shape
        shapes.append(jax.ShapeDtypeStruct((senders,) + block, array.dtype))
        scratch += [
            pltpu.SemaphoreType.DMA((targets,)),
            pltpu.SemaphoreType.DMA((senders,)),
            pltpu.SemaphoreType.DMA(()),
        ]
    return pl.pallas_call(
        functools.partial(exchange_kernel, kinds, sizes),
        out_shape=shapes,
        in_specs=[pl.BlockSpec(memory_space=pltpu.VMEM)] * len(arrays),
        out_specs=[pl.BlockSpec(memory_space=pltpu.VMEM)] * len(arrays),
        scratch_shapes=scratch,
        compiler_params=pltpu.CompilerParams(
            collective_id=collective_id, has_side_effects=True
        ),
        name=name,
    )(*arrays)


def place(dp, y, z):
    return {"dp": dp, "y": y, "z": z}


def coordinates():
    return lax.axis_index("dp"), lax.axis_index("y"), lax.axis_index("z")


def push(src, dst, send_sem, recv_sem, device):
    return pltpu.make_async_remote_copy(
        src_ref=src, dst_ref=dst, send_sem=send_sem, recv_sem=recv_sem,
        device_id=device, device_id_type=pl.DeviceIdType.MESH,
    )


def others(n, own, body):
    def step(i, carry):
        body(lax.rem(own + i, n))
        return carry

    lax.fori_loop(1, n, step, 0)


def greet_rings(sizes):
    dp, y, z = coordinates()
    ndp, ny, nz = sizes
    barrier = pltpu.get_barrier_semaphore()

    def hello(device):
        pl.semaphore_signal(barrier, inc=1, device_id=device, device_id_type=pl.DeviceIdType.MESH)

    others(nz, z, lambda j: hello(place(dp, y, j)))
    others(ny, y, lambda j: hello(place(dp, j, z)))
    others(ndp, dp, lambda j: hello(place(j, y, z)))
    pl.semaphore_wait(barrier, nz + ny + ndp - 3)


def fetch_kernel(sizes, ad, kv, packet, facts, ad_o, kv_o, packet_o, facts_o,
                 z_send, z_recv, y_send, y_recv, x_send, x_recv, mate_send, mate_recv, own_sem):
    dp, y, z = coordinates()
    ndp, ny, nz = sizes
    nx = ndp // 2
    x, core = dp // 2, lax.rem(dp, 2)
    mate = place(2 * x + 1 - core, y, z)

    keep = [
        pltpu.make_async_copy(ad.at[z], ad_o.at[dp, y, z], own_sem.at[0]),
        pltpu.make_async_copy(kv.at[z], kv_o.at[y, z], own_sem.at[1]),
        pltpu.make_async_copy(packet.at[z], packet_o.at[z], own_sem.at[2]),
        pltpu.make_async_copy(facts.at[z], facts_o.at[z], own_sem.at[3]),
    ]
    for copy in keep:
        copy.start()
    greet_rings(sizes)

    def z_copy(item, peer, slot):
        src, dst = [
            (ad.at[peer], ad_o.at[dp, y, slot]),
            (kv.at[peer], kv_o.at[y, slot]),
            (packet.at[peer], packet_o.at[slot]),
            (facts.at[peer], facts_o.at[slot]),
        ][item]
        return push(src, dst, z_send.at[item, peer], z_recv.at[item, slot], place(dp, y, peer))

    def y_copy(item, peer, slot):
        src, dst = [
            (ad_o.at[dp, y], ad_o.at[dp, slot]),
            (kv_o.at[y], kv_o.at[slot]),
        ][item]
        return push(src, dst, y_send.at[item, peer], y_recv.at[item, slot], place(dp, peer, z))

    def x_copy(peer, slot):
        return push(
            ad_o.at[dp], ad_o.at[2 * slot + core], x_send.at[peer], x_recv.at[slot],
            place(2 * peer + core, y, z),
        )

    def mate_copy(block, core_of):
        slot = 2 * block + core_of
        return push(ad_o.at[slot], ad_o.at[slot], mate_send.at[block], mate_recv.at[block], mate)

    for item in range(4):
        others(nz, z, lambda j, item=item: z_copy(item, j, z).start())
    for item in range(2):
        others(nz, z, lambda j, item=item: z_copy(item, j, j).wait_recv())
        keep[item].wait()
        others(ny, y, lambda j, item=item: y_copy(item, j, y).start())
    others(ny, y, lambda j: y_copy(0, j, j).wait_recv())
    others(nx, x, lambda j: x_copy(j, x).start())
    mate_copy(x, core).start()

    def forward(j):
        x_copy(j, j).wait_recv()
        mate_copy(j, core).start()

    others(nx, x, forward)
    for item in (2, 3):
        others(nz, z, lambda j, item=item: z_copy(item, j, j).wait_recv())
        keep[item].wait()
    others(ny, y, lambda j: y_copy(1, j, j).wait_recv())
    mate_copy(x, 1 - core).wait_recv()
    others(nx, x, lambda j: mate_copy(j, 1 - core).wait_recv())
    for item in range(4):
        others(nz, z, lambda j, item=item: z_copy(item, j, z).wait_send())
    for item in range(2):
        others(ny, y, lambda j, item=item: y_copy(item, j, y).wait_send())
    others(nx, x, lambda j: x_copy(j, x).wait_send())
    mate_copy(x, core).wait_send()
    others(nx, x, lambda j: mate_copy(j, core).wait_send())


def fetch(sizes, ad, kv, packet, facts):
    ndp, ny, nz = sizes
    shape = jax.ShapeDtypeStruct
    dma = pltpu.SemaphoreType.DMA
    vmem = pl.BlockSpec(memory_space=pltpu.VMEM)
    return pl.pallas_call(
        functools.partial(fetch_kernel, sizes),
        out_shape=[
            shape((ndp, ny) + ad.shape, ad.dtype),
            shape((ny,) + kv.shape, kv.dtype),
            shape(packet.shape, packet.dtype),
            shape(facts.shape, facts.dtype),
        ],
        in_specs=[vmem] * 4,
        out_specs=[vmem] * 4,
        scratch_shapes=[
            dma((4, nz)), dma((4, nz)), dma((2, ny)), dma((2, ny)), dma((ndp,)), dma((ndp,)),
            dma((ndp,)), dma((ndp,)), dma((4,)),
        ],
        compiler_params=pltpu.CompilerParams(collective_id=1, has_side_effects=True),
        name="fetch",
    )(ad, kv, packet, facts)


def settle_kernel(sizes, terms, out, got, total, mid, send, recv, own_sem):
    dp, y, z = coordinates()
    ndp, ny, nz = sizes
    greet_rings(sizes)

    def share_copy(peer, slot):
        return push(terms.at[peer], got.at[slot], send.at[0, peer], recv.at[0, slot], place(peer, y, z))

    def z_copy(peer, slot):
        return push(total.at[:, peer], mid.at[slot], send.at[1, peer], recv.at[1, slot], place(dp, y, peer))

    def y_copy(peer, slot):
        return push(mid.at[:, peer], out.at[dp, slot], send.at[2, peer], recv.at[2, slot], place(dp, peer, z))

    def spread_copy(peer, slot):
        return push(out.at[dp], out.at[slot], send.at[3, peer], recv.at[3, slot], place(peer, y, z))

    others(ndp, dp, lambda j: share_copy(j, dp).start())
    acc = terms[dp].astype(jnp.float32)
    others(ndp, dp, lambda j: share_copy(j, j).wait_recv())
    for step in range(1, ndp):
        acc += got[lax.rem(dp + step, ndp)].astype(jnp.float32)
    total[...] = acc.astype(total.dtype)
    others(nz, z, lambda j: z_copy(j, z).start())
    mine = pltpu.make_async_copy(total.at[:, z], mid.at[z], own_sem.at[0])
    mine.start()
    others(nz, z, lambda j: z_copy(j, j).wait_recv())
    mine.wait()
    others(ny, y, lambda j: y_copy(j, y).start())
    mine = pltpu.make_async_copy(mid.at[:, y], out.at[dp, y], own_sem.at[1])
    mine.start()
    others(ny, y, lambda j: y_copy(j, j).wait_recv())
    mine.wait()
    others(ndp, dp, lambda j: spread_copy(j, dp).start())
    others(ndp, dp, lambda j: spread_copy(j, j).wait_recv())
    others(ndp, dp, lambda j: share_copy(j, dp).wait_send())
    others(nz, z, lambda j: z_copy(j, z).wait_send())
    others(ny, y, lambda j: y_copy(j, y).wait_send())
    others(ndp, dp, lambda j: spread_copy(j, dp).wait_send())


def settle(sizes, terms):
    ndp, ny, nz = sizes
    most = max(sizes)
    block = terms.shape[3:]
    vmem = pl.BlockSpec(memory_space=pltpu.VMEM)
    return pl.pallas_call(
        functools.partial(settle_kernel, sizes),
        out_shape=jax.ShapeDtypeStruct(terms.shape, terms.dtype),
        in_specs=[vmem],
        out_specs=vmem,
        scratch_shapes=[
            pltpu.VMEM(terms.shape, terms.dtype),
            pltpu.VMEM((ny, nz) + block, terms.dtype),
            pltpu.VMEM((nz, ny) + block, terms.dtype),
            pltpu.SemaphoreType.DMA((4, most)),
            pltpu.SemaphoreType.DMA((4, most)),
            pltpu.SemaphoreType.DMA((2,)),
        ],
        compiler_params=pltpu.CompilerParams(collective_id=5, has_side_effects=True),
        name="settle",
    )(terms)


def compress(keys, values, learned):
    tokens = keys.shape[0]
    k = keys.reshape(tokens, KEY_VALUE_HEADS, HEAD_SIZE)
    v = values.reshape(tokens, KEY_VALUE_HEADS, HEAD_SIZE)
    c = learned.reshape(COMPRESSED_ROWS, KEY_VALUE_HEADS, HEAD_SIZE)
    score = jnp.einsum("cpf,ipf->pci", c, k, preferred_element_type=jnp.float32) * SOFTMAX_SCALE
    weight = jax.nn.softmax(score, axis=-1).astype(jnp.bfloat16)
    short = lambda rows: jnp.einsum(
        "wio,owx->wix", weight, rows, preferred_element_type=jnp.float32
    ).astype(jnp.bfloat16)
    return short(k), short(v)


def attend_local(queries, keys, values, offset):
    slots, tokens = queries.shape[0], keys.shape[0]
    q = queries.reshape(slots, KEY_VALUE_HEADS, GROUP, HEAD_SIZE)
    k = keys.reshape(tokens, KEY_VALUE_HEADS, HEAD_SIZE)
    v = values.reshape(tokens, KEY_VALUE_HEADS, HEAD_SIZE)
    score = jnp.einsum("shgd,nhd->hsgn", q, k, preferred_element_type=jnp.float32) * SOFTMAX_SCALE
    position = offset + jnp.arange(slots, dtype=jnp.int32)
    seen = jnp.arange(tokens, dtype=jnp.int32)[None, :] <= position[:, None]
    seen = seen[None, :, None, :]
    score = jnp.where(seen, score, NEGATIVE_FLOOR)
    peak = jnp.max(score, axis=-1)
    prob = jnp.where(seen, jnp.exp(score - peak[..., None]), 0.0)
    total = jnp.sum(prob, axis=-1)
    acc = jnp.einsum(
        "hsgn,nhd->hsgd", prob.astype(jnp.bfloat16), v, preferred_element_type=jnp.float32
    )
    out = (acc / total[..., None]).astype(jnp.bfloat16)
    return out.reshape(KEY_VALUE_HEADS, slots, GROUP * HEAD_SIZE), peak + jnp.log(total)


def shards(sizes, queries, keys, values, learned, span_len, span_offset, destination, cotangent,
           adapter_a, adapter_b):
    ndp, ny, nz = sizes
    decoders = ny * nz
    model = queries.shape[1]
    wide = model // nz
    narrow = wide // ny
    rows = nz * SLOTS
    dp, y = lax.axis_index("dp"), lax.axis_index("y")

    live = (jnp.arange(SLOTS, dtype=jnp.int32) < span_len[0, 0])[:, None]
    dy = jnp.where(live, cotangent, jnp.zeros_like(cotangent))
    ck, cv = compress(keys, values, learned)
    out_local, lse = attend_local(queries, keys, values, span_offset[0, 0])
    by_head = lambda array: array.reshape(SLOTS, nz, wide).transpose(1, 0, 2)
    packet = jnp.concatenate([by_head(queries), by_head(dy), out_local], axis=-1)
    facts = jnp.concatenate([destination.astype(jnp.float32), live.astype(jnp.float32)], axis=1)
    facts = jnp.concatenate([lse, jnp.broadcast_to(facts[None], (nz, SLOTS, 2))], axis=-1)
    facts = jnp.pad(facts, ((0, 0), (0, 0), (0, 128 - facts.shape[-1])))
    quarters = wide // 128
    chunks = jnp.stack([adapter_a[0], adapter_b[0]]).reshape(2, RANK, nz, quarters, 128)
    chunks = chunks.transpose(0, 3, 2, 1, 4).reshape(2 * quarters, nz, RANK, 128)
    share = 2 * quarters // ndp
    ad = lax.dynamic_slice_in_dim(chunks, dp * share, share, 0)
    ad = ad.transpose(1, 0, 2, 3).reshape(nz, share * RANK, 128)

    ad, short, packet, facts = fetch(
        sizes, ad, jnp.concatenate([ck, cv], axis=-1), packet, facts
    )
    ad = ad.reshape(ndp, decoders, share, RANK, 128)
    if share > 1:
        ad = ad.transpose(0, 2, 1, 3, 4)
    ad = ad.reshape(2, quarters, decoders * RANK, 128)
    downs, ups = ad[0], ad[1]
    packet = packet.reshape(rows, -1)
    facts = facts.reshape(rows, -1)
    q, dy, out_local = packet[:, :wide], packet[:, wide : 2 * wide], packet[:, 2 * wide : 3 * wide]
    short = short.reshape(ny * rows, 2 * HEAD_SIZE)
    ck, cv = short[:, :HEAD_SIZE], short[:, HEAD_SIZE:]
    lse, target, live = facts[:, :GROUP], facts[:, GROUP : GROUP + 1], facts[:, GROUP + 1 : GROUP + 2]

    heads = q.reshape(rows, GROUP, HEAD_SIZE)
    score = jnp.einsum("rgd,kd->grk", heads, ck, preferred_element_type=jnp.float32) * SOFTMAX_SCALE
    segment = y * nz + jnp.arange(rows, dtype=jnp.int32) // SLOTS
    source = jnp.arange(ny * rows, dtype=jnp.int32) // COMPRESSED_ROWS
    seen = (source[None, :] < segment[:, None])[None]
    score = jnp.where(seen, score, NEGATIVE_FLOOR)
    lse = lse.T
    peak = jnp.maximum(lse, jnp.max(score, axis=-1))
    prob = jnp.where(seen, jnp.exp(score - peak[..., None]), 0.0)
    weight = jnp.exp(lse - peak)
    total = weight + jnp.sum(prob, axis=-1)
    acc = jnp.einsum(
        "grk,kd->grd", prob.astype(jnp.bfloat16), cv, preferred_element_type=jnp.float32
    )
    home = out_local.reshape(rows, GROUP, HEAD_SIZE).transpose(1, 0, 2).astype(jnp.float32)
    attn = (acc + weight[..., None] * home) / total[..., None]
    attn = attn.transpose(1, 0, 2).reshape(rows, wide)
    attn = jnp.where(live > 0.5, attn, 0.0).astype(jnp.bfloat16)

    column = jnp.arange(decoders * RANK, dtype=jnp.int32)
    column_decoder, column_rank = column // RANK, column % RANK
    own = target.astype(jnp.int32) == column_decoder[None, :]
    pick = column_rank[:, None] == jnp.arange(RANK, dtype=jnp.int32)[None, :]
    across = (((1,), (1,)), ((), ()))

    def narrowed(left, right):
        full = sum(
            lax.dot_general(
                left[:, 128 * i : 128 * (i + 1)], right[i], across,
                preferred_element_type=jnp.float32,
            )
            for i in range(quarters)
        )
        return lax.dot_general(
            pick.astype(jnp.float32), jnp.where(own, full, 0.0), (((0,), (1,)), ((), ())),
            precision=HIGH, preferred_element_type=jnp.float32,
        )

    x = attn.astype(jnp.float32)
    square = jnp.sum(x * x, axis=1)[None]
    partial = jnp.concatenate(
        [narrowed(attn, downs), narrowed(dy, ups), square, jnp.zeros((7, rows), jnp.float32)], axis=0
    )
    (partial,) = exchange("sums", 3, sizes, (partial, "z_spread"))
    sums = jnp.sum(partial, axis=0)
    rs = lax.rsqrt(sums[2 * RANK : 2 * RANK + 1] / model + EPS)
    hid_exact = sums[:RANK] * rs
    hid = hid_exact.astype(jnp.bfloat16)
    back = (SCALE * sums[RANK : 2 * RANK]).astype(jnp.bfloat16)
    dot_mean = jnp.sum(back.astype(jnp.float32) * hid_exact, axis=0, keepdims=True) / model
    rs_column, mean_column = rs.T, dot_mean.T
    spread = lax.dot_general(
        back, pick.astype(jnp.bfloat16), (((0,), (1,)), ((), ())), preferred_element_type=jnp.float32
    )
    spread = jnp.where(own, spread, 0.0).astype(jnp.bfloat16)
    dn = jnp.concatenate(
        [jnp.dot(spread, downs[i], preferred_element_type=jnp.float32) for i in range(quarters)], axis=1
    )
    nrm = x * rs_column
    d_rows = (dy.astype(jnp.float32) + rs_column * (dn - nrm * mean_column)).astype(jnp.bfloat16)
    normed = nrm.astype(jnp.bfloat16)

    slices = lambda array: array.reshape(rows, ny, narrow).transpose(1, 0, 2)
    columns = jnp.concatenate([slices(normed), slices(dy)], axis=-1)
    small = jnp.concatenate(
        [hid, back, jnp.broadcast_to(target.T, (RANK, rows)).astype(jnp.bfloat16)], axis=0
    )
    d_rows, columns, small = exchange(
        "rows", 4, sizes,
        (d_rows.reshape(nz, SLOTS, wide), "z_swap"), (columns, "y_swap"), (small, "y_spread"),
    )
    grad_rows = d_rows.transpose(1, 0, 2).reshape(SLOTS, model)
    columns = columns.reshape(ny * rows, 2 * narrow)
    small = small.transpose(1, 0, 2).reshape(3 * RANK, ny * rows)
    chosen = (
        small[2 * RANK].astype(jnp.int32)[None, :]
        == jnp.arange(decoders, dtype=jnp.int32)[:, None]
    )[:, None, :]

    def gathered(values_):
        left = jnp.where(chosen, values_[None], jnp.zeros((), jnp.bfloat16))
        return jnp.dot(
            left.reshape(decoders * RANK, ny * rows), columns, preferred_element_type=jnp.float32
        )

    from_hid = SCALE * gathered(small[:RANK])
    from_back = gathered(small[RANK : 2 * RANK])
    is_a = (jnp.arange(2 * narrow, dtype=jnp.int32) < narrow)[None, :]
    terms = jnp.where(is_a, from_back, from_hid).astype(jnp.bfloat16)
    terms = terms.reshape(ny, nz, ndp, RANK // ndp, 2 * narrow).transpose(2, 0, 1, 3, 4)
    grads = settle(sizes, terms)
    grads = grads.reshape(ndp, ny, nz, RANK // ndp, 2, narrow).transpose(4, 0, 3, 2, 1, 5)
    grads = grads.astype(jnp.float32)
    grads = grads.reshape(2, 1, RANK, model)
    return grad_rows, grads[0], grads[1]


def solution(mesh):
    ndp, nctx = mesh.devices.shape
    nz = KEY_VALUE_HEADS
    sizes = (ndp, nctx // nz, nz)
    fine = Mesh(mesh.devices.reshape(sizes), ("dp", "y", "z"))
    ctx = ("y", "z")
    both = ("dp", "y", "z")
    in_specs = (
        P(both, None),
        P(both, None),
        P(both, None),
        P(),
        P("dp", ctx),
        P("dp", ctx),
        P(both, None),
        P(both, None),
        P(ctx, None, None),
        P(ctx, None, None),
    )
    out_specs = (P(both, None), P(ctx, None, None), P(ctx, None, None))
    return jax.shard_map(
        functools.partial(shards, sizes), mesh=fine, in_specs=in_specs, out_specs=out_specs,
        check_vma=False,
    )
```

```python
import functools
import math

import jax
import jax.numpy as jnp
from jax import lax
from jax.experimental import pallas as pl
from jax.experimental.pallas import tpu as pltpu
from jax.sharding import Mesh
from jax.sharding import PartitionSpec as P

QUERY_HEADS = 32
KEY_VALUE_HEADS = 8
GROUP = QUERY_HEADS // KEY_VALUE_HEADS
HEAD_SIZE = 128
COMPRESSED_ROWS = 16
RANK = 16
SLOTS = 16

SCALE = 2.0
EPS = 1e-06
NEGATIVE_FLOOR = -1e30
SOFTMAX_SCALE = 1.0 / math.sqrt(HEAD_SIZE)
HIGH = lax.Precision.HIGHEST


def routes(kind, sizes, me):
    dp, y, z = me
    ndp, ny, nz = sizes
    if kind == "plane":
        def route(i):
            yy, zz = i // nz, i % nz
            return {"dp": dp, "y": yy, "z": zz}, zz
        return ny * nz, route, y * nz + z
    if kind == "owners":
        def route(i):
            pp, zz = i // nz, i % nz
            return {"dp": pp, "y": dp, "z": zz}, zz
        return ndp * nz, route, y * nz + z
    axis, form = kind.split("_")
    n = {"dp": ndp, "y": ny, "z": nz}[axis]
    own = {"dp": dp, "y": y, "z": z}[axis]

    def route(i):
        where = {"dp": dp, "y": y, "z": z}
        where[axis] = i
        return where, (i if form == "swap" else None)

    return n, route, own


def exchange_kernel(kinds, sizes, *refs):
    n_items = len(kinds)
    ins, outs = refs[:n_items], refs[n_items : 2 * n_items]
    sems = refs[2 * n_items :]
    me = (lax.axis_index("dp"), lax.axis_index("y"), lax.axis_index("z"))
    dp, y, z = me
    ndp, ny, nz = sizes
    barrier = pltpu.get_barrier_semaphore()
    owners = "owners" in kinds

    greeted = []
    if "plane" in kinds:
        greeted.append("plane")
    for axis in ("z", "y", "dp"):
        if any(kind.startswith(axis + "_") for kind in kinds):
            if not (axis in ("y", "z") and "plane" in kinds):
                greeted.append(axis + "_spread")
    expected = 0
    for kind in greeted:
        n, route, own = routes(kind, sizes, me)

        def greet(step, carry, n=n, route=route, own=own):
            device, _ = route(lax.rem(own + step, n))
            pl.semaphore_signal(
                barrier, inc=1, device_id=device, device_id_type=pl.DeviceIdType.MESH
            )
            return carry

        lax.fori_loop(1, n, greet, 0)
        expected += n - 1
    if owners:
        mine = dp == y

        def greet_sender(i, carry):
            yy, zz = i // nz, lax.rem(i, nz)

            @pl.when(jnp.logical_not(mine & (yy == y) & (zz == z)))
            def _():
                pl.semaphore_signal(
                    barrier,
                    inc=1,
                    device_id={"dp": y, "y": yy, "z": zz},
                    device_id_type=pl.DeviceIdType.MESH,
                )

            return carry

        lax.fori_loop(0, ny * nz, greet_sender, 0)
        pl.semaphore_wait(barrier, ndp * nz - mine.astype(jnp.int32))
    if expected:
        pl.semaphore_wait(barrier, expected)

    def remote(item, i):
        kind = kinds[item]
        n, route, own = routes(kind, sizes, me)
        device, block = route(i)
        src = ins[item] if block is None else ins[item].at[block]
        return pltpu.make_async_remote_copy(
            src_ref=src,
            dst_ref=outs[item].at[own],
            send_sem=sems[3 * item].at[i],
            recv_sem=sems[3 * item + 1].at[own],
            device_id=device,
            device_id_type=pl.DeviceIdType.MESH,
        )

    def arrival(item, i):
        kind = kinds[item]
        block = None if kind.endswith("spread") else 0
        src = ins[item] if block is None else ins[item].at[block]
        return pltpu.make_async_remote_copy(
            src_ref=src,
            dst_ref=outs[item].at[i],
            send_sem=sems[3 * item].at[i],
            recv_sem=sems[3 * item + 1].at[i],
            device_id={"dp": dp, "y": y, "z": z},
            device_id_type=pl.DeviceIdType.MESH,
        )

    def local(item):
        kind = kinds[item]
        n, route, own = routes(kind, sizes, me)
        if kind in ("plane", "owners"):
            block = z
        else:
            block = own if kind.endswith("swap") else None
        src = ins[item] if block is None else ins[item].at[block]
        return pltpu.make_async_copy(src, outs[item].at[own], sems[3 * item + 2])

    for item, kind in enumerate(kinds):
        n, route, own = routes(kind, sizes, me)
        if kind == "owners":
            def send(i, carry, item=item):
                self_here = mine & (i == dp * nz + z)

                @pl.when(self_here)
                def _():
                    local(item).start()

                @pl.when(jnp.logical_not(self_here))
                def _():
                    remote(item, i).start()

                return carry

            lax.fori_loop(0, n, send, 0)
        else:
            def send(step, carry, item=item, n=n, own=own):
                remote(item, lax.rem(own + step, n)).start()
                return carry

            lax.fori_loop(1, n, send, 0)
            local(item).start()

    for item, kind in enumerate(kinds):
        n, route, own = routes(kind, sizes, me)
        if kind == "owners":
            def finish(i, carry, item=item):
                @pl.when(jnp.logical_not(mine & (i == dp * nz + z)))
                def _():
                    remote(item, i).wait_send()

                return carry

            lax.fori_loop(0, n, finish, 0)

            def collect(i, carry, item=item):
                @pl.when(jnp.logical_not(mine & (i == y * nz + z)))
                def _():
                    arrival(item, i).wait_recv()

                return carry

            lax.fori_loop(0, ny * nz, collect, 0)

            @pl.when(mine)
            def _(item=item):
                local(item).wait()
        else:
            def finish(step, carry, item=item, n=n, own=own):
                peer = lax.rem(own + step, n)
                remote(item, peer).wait_send()
                arrival(item, peer).wait_recv()
                return carry

            lax.fori_loop(1, n, finish, 0)
            local(item).wait()


def exchange(name, collective_id, sizes, *items):
    arrays = [item[0] for item in items]
    kinds = tuple(item[1] for item in items)
    ndp, ny, nz = sizes
    shapes, scratch = [], []
    for array, kind in zip(arrays, kinds):
        if kind in ("plane", "owners"):
            senders, targets = ny * nz, (ny * nz if kind == "plane" else ndp * nz)
            block = array.shape[1:]
        else:
            senders = targets = {"dp": ndp, "y": ny, "z": nz}[kind.split("_")[0]]
            block = array.shape[1:] if kind.endswith("swap") else array.shape
        shapes.append(jax.ShapeDtypeStruct((senders,) + block, array.dtype))
        scratch += [
            pltpu.SemaphoreType.DMA((targets,)),
            pltpu.SemaphoreType.DMA((senders,)),
            pltpu.SemaphoreType.DMA(()),
        ]
    return pl.pallas_call(
        functools.partial(exchange_kernel, kinds, sizes),
        out_shape=shapes,
        in_specs=[pl.BlockSpec(memory_space=pltpu.VMEM)] * len(arrays),
        out_specs=[pl.BlockSpec(memory_space=pltpu.VMEM)] * len(arrays),
        scratch_shapes=scratch,
        compiler_params=pltpu.CompilerParams(
            collective_id=collective_id, has_side_effects=True
        ),
        name=name,
    )(*arrays)


def place(dp, y, z):
    return {"dp": dp, "y": y, "z": z}


def coordinates():
    return lax.axis_index("dp"), lax.axis_index("y"), lax.axis_index("z")


def push(src, dst, send_sem, recv_sem, device):
    return pltpu.make_async_remote_copy(
        src_ref=src, dst_ref=dst, send_sem=send_sem, recv_sem=recv_sem,
        device_id=device, device_id_type=pl.DeviceIdType.MESH,
    )


def others(n, own, body):
    def step(i, carry):
        body(lax.rem(own + i, n))
        return carry

    lax.fori_loop(1, n, step, 0)


def greet_rings(sizes):
    dp, y, z = coordinates()
    ndp, ny, nz = sizes
    barrier = pltpu.get_barrier_semaphore()

    def hello(device):
        pl.semaphore_signal(barrier, inc=1, device_id=device, device_id_type=pl.DeviceIdType.MESH)

    others(nz, z, lambda j: hello(place(dp, y, j)))
    others(ny, y, lambda j: hello(place(dp, j, z)))
    others(ndp, dp, lambda j: hello(place(j, y, z)))
    pl.semaphore_wait(barrier, nz + ny + ndp - 3)


def fetch_kernel(sizes, ad, kv, packet, facts, ad_o, kv_o, packet_o, facts_o,
                 z_send, z_recv, y_send, y_recv, x_send, x_recv, mate_send, mate_recv, own_sem):
    dp, y, z = coordinates()
    ndp, ny, nz = sizes
    nx = ndp // 2
    x, core = dp // 2, lax.rem(dp, 2)
    mate = place(2 * x + 1 - core, y, z)

    keep = [
        pltpu.make_async_copy(ad.at[z], ad_o.at[dp, y, z], own_sem.at[0]),
        pltpu.make_async_copy(kv.at[z], kv_o.at[y, z], own_sem.at[1]),
        pltpu.make_async_copy(packet.at[z], packet_o.at[z], own_sem.at[2]),
        pltpu.make_async_copy(facts.at[z], facts_o.at[z], own_sem.at[3]),
    ]
    for copy in keep:
        copy.start()
    greet_rings(sizes)

    def z_copy(item, peer, slot):
        src, dst = [
            (ad.at[peer], ad_o.at[dp, y, slot]),
            (kv.at[peer], kv_o.at[y, slot]),
            (packet.at[peer], packet_o.at[slot]),
            (facts.at[peer], facts_o.at[slot]),
        ][item]
        return push(src, dst, z_send.at[item, peer], z_recv.at[item, slot], place(dp, y, peer))

    def y_copy(item, peer, slot):
        src, dst = [
            (ad_o.at[dp, y], ad_o.at[dp, slot]),
            (kv_o.at[y], kv_o.at[slot]),
        ][item]
        return push(src, dst, y_send.at[item, peer], y_recv.at[item, slot], place(dp, peer, z))

    def x_copy(peer, slot):
        return push(
            ad_o.at[dp], ad_o.at[2 * slot + core], x_send.at[peer], x_recv.at[slot],
            place(2 * peer + core, y, z),
        )

    def mate_copy(block, core_of):
        slot = 2 * block + core_of
        return push(ad_o.at[slot], ad_o.at[slot], mate_send.at[block], mate_recv.at[block], mate)

    for item in range(4):
        others(nz, z, lambda j, item=item: z_copy(item, j, z).start())
    for item in range(2):
        others(nz, z, lambda j, item=item: z_copy(item, j, j).wait_recv())
        keep[item].wait()
        others(ny, y, lambda j, item=item: y_copy(item, j, y).start())
    others(ny, y, lambda j: y_copy(0, j, j).wait_recv())
    others(nx, x, lambda j: x_copy(j, x).start())
    mate_copy(x, core).start()

    def forward(j):
        x_copy(j, j).wait_recv()
        mate_copy(j, core).start()

    others(nx, x, forward)
    for item in (2, 3):
        others(nz, z, lambda j, item=item: z_copy(item, j, j).wait_recv())
        keep[item].wait()
    others(ny, y, lambda j: y_copy(1, j, j).wait_recv())
    mate_copy(x, 1 - core).wait_recv()
    others(nx, x, lambda j: mate_copy(j, 1 - core).wait_recv())
    for item in range(4):
        others(nz, z, lambda j, item=item: z_copy(item, j, z).wait_send())
    for item in range(2):
        others(ny, y, lambda j, item=item: y_copy(item, j, y).wait_send())
    others(nx, x, lambda j: x_copy(j, x).wait_send())
    mate_copy(x, core).wait_send()
    others(nx, x, lambda j: mate_copy(j, core).wait_send())


def fetch(sizes, ad, kv, packet, facts):
    ndp, ny, nz = sizes
    shape = jax.ShapeDtypeStruct
    dma = pltpu.SemaphoreType.DMA
    vmem = pl.BlockSpec(memory_space=pltpu.VMEM)
    return pl.pallas_call(
        functools.partial(fetch_kernel, sizes),
        out_shape=[
            shape((ndp, ny) + ad.shape, ad.dtype),
            shape((ny,) + kv.shape, kv.dtype),
            shape(packet.shape, packet.dtype),
            shape(facts.shape, facts.dtype),
        ],
        in_specs=[vmem] * 4,
        out_specs=[vmem] * 4,
        scratch_shapes=[
            dma((4, nz)), dma((4, nz)), dma((2, ny)), dma((2, ny)), dma((ndp,)), dma((ndp,)),
            dma((ndp,)), dma((ndp,)), dma((4,)),
        ],
        compiler_params=pltpu.CompilerParams(collective_id=1, has_side_effects=True),
        name="fetch",
    )(ad, kv, packet, facts)


def settle_kernel(sizes, terms, out, got, total, mid, send, recv, own_sem):
    dp, y, z = coordinates()
    ndp, ny, nz = sizes
    greet_rings(sizes)

    def share_copy(peer, slot):
        return push(terms.at[peer], got.at[slot], send.at[0, peer], recv.at[0, slot], place(peer, y, z))

    def z_copy(peer, slot):
        return push(total.at[:, peer], mid.at[slot], send.at[1, peer], recv.at[1, slot], place(dp, y, peer))

    def y_copy(peer, slot):
        return push(mid.at[:, peer], out.at[dp, slot], send.at[2, peer], recv.at[2, slot], place(dp, peer, z))

    def spread_copy(peer, slot):
        return push(out.at[dp], out.at[slot], send.at[3, peer], recv.at[3, slot], place(peer, y, z))

    others(ndp, dp, lambda j: share_copy(j, dp).start())
    acc = terms[dp].astype(jnp.float32)
    others(ndp, dp, lambda j: share_copy(j, j).wait_recv())
    for step in range(1, ndp):
        acc += got[lax.rem(dp + step, ndp)].astype(jnp.float32)
    total[...] = acc.astype(total.dtype)
    others(nz, z, lambda j: z_copy(j, z).start())
    mine = pltpu.make_async_copy(total.at[:, z], mid.at[z], own_sem.at[0])
    mine.start()
    others(nz, z, lambda j: z_copy(j, j).wait_recv())
    mine.wait()
    others(ny, y, lambda j: y_copy(j, y).start())
    mine = pltpu.make_async_copy(mid.at[:, y], out.at[dp, y], own_sem.at[1])
    mine.start()
    others(ny, y, lambda j: y_copy(j, j).wait_recv())
    mine.wait()
    others(ndp, dp, lambda j: spread_copy(j, dp).start())
    others(ndp, dp, lambda j: spread_copy(j, j).wait_recv())
    others(ndp, dp, lambda j: share_copy(j, dp).wait_send())
    others(nz, z, lambda j: z_copy(j, z).wait_send())
    others(ny, y, lambda j: y_copy(j, y).wait_send())
    others(ndp, dp, lambda j: spread_copy(j, dp).wait_send())


def settle(sizes, terms):
    ndp, ny, nz = sizes
    most = max(sizes)
    block = terms.shape[3:]
    vmem = pl.BlockSpec(memory_space=pltpu.VMEM)
    return pl.pallas_call(
        functools.partial(settle_kernel, sizes),
        out_shape=jax.ShapeDtypeStruct(terms.shape, terms.dtype),
        in_specs=[vmem],
        out_specs=vmem,
        scratch_shapes=[
            pltpu.VMEM(terms.shape, terms.dtype),
            pltpu.VMEM((ny, nz) + block, terms.dtype),
            pltpu.VMEM((nz, ny) + block, terms.dtype),
            pltpu.SemaphoreType.DMA((4, most)),
            pltpu.SemaphoreType.DMA((4, most)),
            pltpu.SemaphoreType.DMA((2,)),
        ],
        compiler_params=pltpu.CompilerParams(collective_id=5, has_side_effects=True),
        name="settle",
    )(terms)


def compress(keys, values, learned):
    tokens = keys.shape[0]
    k = keys.reshape(tokens, KEY_VALUE_HEADS, HEAD_SIZE)
    v = values.reshape(tokens, KEY_VALUE_HEADS, HEAD_SIZE)
    c = learned.reshape(COMPRESSED_ROWS, KEY_VALUE_HEADS, HEAD_SIZE)
    score = jnp.einsum("cpf,ipf->pci", c, k, preferred_element_type=jnp.float32) * SOFTMAX_SCALE
    weight = jax.nn.softmax(score, axis=-1).astype(jnp.bfloat16)
    short = lambda rows: jnp.einsum(
        "wio,owx->wix", weight, rows, preferred_element_type=jnp.float32
    ).astype(jnp.bfloat16)
    return short(k), short(v)


def attend_local(queries, keys, values, offset):
    slots, tokens = queries.shape[0], keys.shape[0]
    q = queries.reshape(slots, KEY_VALUE_HEADS, GROUP, HEAD_SIZE)
    k = keys.reshape(tokens, KEY_VALUE_HEADS, HEAD_SIZE)
    v = values.reshape(tokens, KEY_VALUE_HEADS, HEAD_SIZE)
    score = jnp.einsum("shgd,nhd->hsgn", q, k, preferred_element_type=jnp.float32) * SOFTMAX_SCALE
    position = offset + jnp.arange(slots, dtype=jnp.int32)
    seen = jnp.arange(tokens, dtype=jnp.int32)[None, :] <= position[:, None]
    seen = seen[None, :, None, :]
    score = jnp.where(seen, score, NEGATIVE_FLOOR)
    peak = jnp.max(score, axis=-1)
    prob = jnp.where(seen, jnp.exp(score - peak[..., None]), 0.0)
    total = jnp.sum(prob, axis=-1)
    acc = jnp.einsum(
        "hsgn,nhd->hsgd", prob.astype(jnp.bfloat16), v, preferred_element_type=jnp.float32
    )
    out = (acc / total[..., None]).astype(jnp.bfloat16)
    return out.reshape(KEY_VALUE_HEADS, slots, GROUP * HEAD_SIZE), peak + jnp.log(total)


def shards(sizes, queries, keys, values, learned, span_len, span_offset, destination, cotangent,
           adapter_a, adapter_b):
    ndp, ny, nz = sizes
    decoders = ny * nz
    model = queries.shape[1]
    wide = model // nz
    narrow = wide // ny
    rows = nz * SLOTS
    dp, y = lax.axis_index("dp"), lax.axis_index("y")

    live = (jnp.arange(SLOTS, dtype=jnp.int32) < span_len[0, 0])[:, None]
    dy = jnp.where(live, cotangent, jnp.zeros_like(cotangent))
    ck, cv = compress(keys, values, learned)
    out_local, lse = attend_local(queries, keys, values, span_offset[0, 0])
    by_head = lambda array: array.reshape(SLOTS, nz, wide).transpose(1, 0, 2)
    packet = jnp.concatenate([by_head(queries), by_head(dy), out_local], axis=-1)
    facts = jnp.concatenate([destination.astype(jnp.float32), live.astype(jnp.float32)], axis=1)
    facts = jnp.concatenate([lse, jnp.broadcast_to(facts[None], (nz, SLOTS, 2))], axis=-1)
    facts = jnp.pad(facts, ((0, 0), (0, 0), (0, 128 - facts.shape[-1])))
    quarters = wide // 128
    chunks = jnp.stack([adapter_a[0], adapter_b[0]]).reshape(2, RANK, nz, quarters, 128)
    chunks = chunks.transpose(0, 3, 2, 1, 4).reshape(2 * quarters, nz, RANK, 128)
    share = 2 * quarters // ndp
    ad = lax.dynamic_slice_in_dim(chunks, dp * share, share, 0)
    ad = ad.transpose(1, 0, 2, 3).reshape(nz, share * RANK, 128)

    ad, short, packet, facts = fetch(
        sizes, ad, jnp.concatenate([ck, cv], axis=-1), packet, facts
    )
    ad = ad.reshape(ndp, decoders, share, RANK, 128)
    if share > 1:
        ad = ad.transpose(0, 2, 1, 3, 4)
    ad = ad.reshape(2, quarters, decoders * RANK, 128).transpose(0, 2, 1, 3)
    ad = ad.reshape(2, decoders * RANK, wide)
    downs, ups = ad[0], ad[1]
    packet = packet.reshape(rows, -1)
    facts = facts.reshape(rows, -1)
    q, dy, out_local = packet[:, :wide], packet[:, wide : 2 * wide], packet[:, 2 * wide : 3 * wide]
    short = short.reshape(ny * rows, 2 * HEAD_SIZE)
    ck, cv = short[:, :HEAD_SIZE], short[:, HEAD_SIZE:]
    lse, target, live = facts[:, :GROUP], facts[:, GROUP : GROUP + 1], facts[:, GROUP + 1 : GROUP + 2]

    heads = q.reshape(rows, GROUP, HEAD_SIZE)
    score = jnp.einsum("rgd,kd->grk", heads, ck, preferred_element_type=jnp.float32) * SOFTMAX_SCALE
    segment = y * nz + jnp.arange(rows, dtype=jnp.int32) // SLOTS
    source = jnp.arange(ny * rows, dtype=jnp.int32) // COMPRESSED_ROWS
    seen = (source[None, :] < segment[:, None])[None]
    score = jnp.where(seen, score, NEGATIVE_FLOOR)
    lse = lse.T
    peak = jnp.maximum(lse, jnp.max(score, axis=-1))
    prob = jnp.where(seen, jnp.exp(score - peak[..., None]), 0.0)
    weight = jnp.exp(lse - peak)
    total = weight + jnp.sum(prob, axis=-1)
    acc = jnp.einsum(
        "grk,kd->grd", prob.astype(jnp.bfloat16), cv, preferred_element_type=jnp.float32
    )
    home = out_local.reshape(rows, GROUP, HEAD_SIZE).transpose(1, 0, 2).astype(jnp.float32)
    attn = (acc + weight[..., None] * home) / total[..., None]
    attn = attn.transpose(1, 0, 2).reshape(rows, wide)
    attn = jnp.where(live > 0.5, attn, 0.0).astype(jnp.bfloat16)

    column = jnp.arange(decoders * RANK, dtype=jnp.int32)
    column_decoder, column_rank = column // RANK, column % RANK
    own = target.astype(jnp.int32) == column_decoder[None, :]
    pick = column_rank[:, None] == jnp.arange(RANK, dtype=jnp.int32)[None, :]
    across = (((1,), (1,)), ((), ()))

    def narrowed(left, right):
        full = lax.dot_general(left, right, across, preferred_element_type=jnp.float32)
        return lax.dot_general(
            pick.astype(jnp.float32), jnp.where(own, full, 0.0), (((0,), (1,)), ((), ())),
            precision=HIGH, preferred_element_type=jnp.float32,
        )

    x = attn.astype(jnp.float32)
    square = jnp.sum(x * x, axis=1)[None]
    partial = jnp.concatenate(
        [narrowed(attn, downs), narrowed(dy, ups), square, jnp.zeros((7, rows), jnp.float32)], axis=0
    )
    slices = lambda array: array.reshape(rows, ny, narrow).transpose(1, 0, 2)
    columns = jnp.concatenate([slices(attn), slices(dy)], axis=-1)
    partial, columns = exchange("sums", 3, sizes, (partial, "z_spread"), (columns, "y_swap"))
    sums = jnp.sum(partial, axis=0)
    rs = lax.rsqrt(sums[2 * RANK : 2 * RANK + 1] / model + EPS)
    hid_exact = sums[:RANK] * rs
    hid = hid_exact.astype(jnp.bfloat16)
    back = (SCALE * sums[RANK : 2 * RANK]).astype(jnp.bfloat16)
    dot_mean = jnp.sum(back.astype(jnp.float32) * hid_exact, axis=0, keepdims=True) / model
    rs_column, mean_column = rs.T, dot_mean.T
    spread = lax.dot_general(
        back, pick.astype(jnp.bfloat16), (((0,), (1,)), ((), ())), preferred_element_type=jnp.float32
    )
    spread = jnp.where(own, spread, 0.0).astype(jnp.bfloat16)
    dn = jnp.dot(spread, downs, preferred_element_type=jnp.float32)
    nrm = x * rs_column
    d_rows = (dy.astype(jnp.float32) + rs_column * (dn - nrm * mean_column)).astype(jnp.bfloat16)

    scaled = (back.astype(jnp.float32) * rs).astype(jnp.bfloat16)
    small = jnp.concatenate(
        [hid, scaled, jnp.broadcast_to(target.T, (RANK, rows)).astype(jnp.bfloat16)], axis=0
    )
    d_rows, small = exchange(
        "rows", 4, sizes, (d_rows.reshape(nz, SLOTS, wide), "z_swap"), (small, "y_spread")
    )
    grad_rows = d_rows.transpose(1, 0, 2).reshape(SLOTS, model)
    columns = columns.reshape(ny * rows, 2 * narrow)
    small = small.transpose(1, 0, 2).reshape(3 * RANK, ny * rows)
    chosen = (
        small[2 * RANK].astype(jnp.int32)[None, :]
        == jnp.arange(decoders, dtype=jnp.int32)[:, None]
    )[:, None, :]

    def gathered(values_):
        left = jnp.where(chosen, values_[None], jnp.zeros((), jnp.bfloat16))
        return jnp.dot(
            left.reshape(decoders * RANK, ny * rows), columns, preferred_element_type=jnp.float32
        )

    from_hid = SCALE * gathered(small[:RANK])
    from_back = gathered(small[RANK : 2 * RANK])
    is_a = (jnp.arange(2 * narrow, dtype=jnp.int32) < narrow)[None, :]
    terms = jnp.where(is_a, from_back, from_hid).astype(jnp.bfloat16)
    terms = terms.reshape(ny, nz, ndp, RANK // ndp, 2 * narrow).transpose(2, 0, 1, 3, 4)
    grads = settle(sizes, terms)
    final = lambda part: part.transpose(0, 3, 2, 1, 4).reshape(1, RANK, model).astype(jnp.float32)
    return grad_rows, final(grads[..., :narrow]), final(grads[..., narrow:])


def solution(mesh):
    ndp, nctx = mesh.devices.shape
    nz = KEY_VALUE_HEADS
    sizes = (ndp, nctx // nz, nz)
    fine = Mesh(mesh.devices.reshape(sizes), ("dp", "y", "z"))
    ctx = ("y", "z")
    both = ("dp", "y", "z")
    in_specs = (
        P(both, None),
        P(both, None),
        P(both, None),
        P(),
        P("dp", ctx),
        P("dp", ctx),
        P(both, None),
        P(both, None),
        P(ctx, None, None),
        P(ctx, None, None),
    )
    out_specs = (P(both, None), P(ctx, None, None), P(ctx, None, None))
    return jax.shard_map(
        functools.partial(shards, sizes), mesh=fine, in_specs=in_specs, out_specs=out_specs,
        check_vma=False,
    )
```

```python
import functools
import math

import jax
import jax.numpy as jnp
from jax import lax
from jax.experimental import pallas as pl
from jax.experimental.pallas import tpu as pltpu
from jax.sharding import Mesh
from jax.sharding import PartitionSpec as P

QUERY_HEADS = 32
KEY_VALUE_HEADS = 8
GROUP = QUERY_HEADS // KEY_VALUE_HEADS
HEAD_SIZE = 128
COMPRESSED_ROWS = 16
RANK = 16
SLOTS = 16

SCALE = 2.0
EPS = 1e-06
NEGATIVE_FLOOR = -1e30
SOFTMAX_SCALE = 1.0 / math.sqrt(HEAD_SIZE)
HIGH = lax.Precision.HIGHEST


def routes(kind, sizes, me):
    dp, y, z = me
    ndp, ny, nz = sizes
    if kind == "plane":
        def route(i):
            yy, zz = i // nz, i % nz
            return {"dp": dp, "y": yy, "z": zz}, zz
        return ny * nz, route, y * nz + z
    if kind == "owners":
        def route(i):
            pp, zz = i // nz, i % nz
            return {"dp": pp, "y": dp, "z": zz}, zz
        return ndp * nz, route, y * nz + z
    axis, form = kind.split("_")
    n = {"dp": ndp, "y": ny, "z": nz}[axis]
    own = {"dp": dp, "y": y, "z": z}[axis]

    def route(i):
        where = {"dp": dp, "y": y, "z": z}
        where[axis] = i
        return where, (i if form == "swap" else None)

    return n, route, own


def exchange_kernel(kinds, sizes, *refs):
    n_items = len(kinds)
    ins, outs = refs[:n_items], refs[n_items : 2 * n_items]
    sems = refs[2 * n_items :]
    me = (lax.axis_index("dp"), lax.axis_index("y"), lax.axis_index("z"))
    dp, y, z = me
    ndp, ny, nz = sizes
    barrier = pltpu.get_barrier_semaphore()
    owners = "owners" in kinds

    greeted = []
    if "plane" in kinds:
        greeted.append("plane")
    for axis in ("z", "y", "dp"):
        if any(kind.startswith(axis + "_") for kind in kinds):
            if not (axis in ("y", "z") and "plane" in kinds):
                greeted.append(axis + "_spread")
    expected = 0
    for kind in greeted:
        n, route, own = routes(kind, sizes, me)

        def greet(step, carry, n=n, route=route, own=own):
            device, _ = route(lax.rem(own + step, n))
            pl.semaphore_signal(
                barrier, inc=1, device_id=device, device_id_type=pl.DeviceIdType.MESH
            )
            return carry

        lax.fori_loop(1, n, greet, 0)
        expected += n - 1
    if owners:
        mine = dp == y

        def greet_sender(i, carry):
            yy, zz = i // nz, lax.rem(i, nz)

            @pl.when(jnp.logical_not(mine & (yy == y) & (zz == z)))
            def _():
                pl.semaphore_signal(
                    barrier,
                    inc=1,
                    device_id={"dp": y, "y": yy, "z": zz},
                    device_id_type=pl.DeviceIdType.MESH,
                )

            return carry

        lax.fori_loop(0, ny * nz, greet_sender, 0)
        pl.semaphore_wait(barrier, ndp * nz - mine.astype(jnp.int32))
    if expected:
        pl.semaphore_wait(barrier, expected)

    def remote(item, i):
        kind = kinds[item]
        n, route, own = routes(kind, sizes, me)
        device, block = route(i)
        src = ins[item] if block is None else ins[item].at[block]
        return pltpu.make_async_remote_copy(
            src_ref=src,
            dst_ref=outs[item].at[own],
            send_sem=sems[3 * item].at[i],
            recv_sem=sems[3 * item + 1].at[own],
            device_id=device,
            device_id_type=pl.DeviceIdType.MESH,
        )

    def arrival(item, i):
        kind = kinds[item]
        block = None if kind.endswith("spread") else 0
        src = ins[item] if block is None else ins[item].at[block]
        return pltpu.make_async_remote_copy(
            src_ref=src,
            dst_ref=outs[item].at[i],
            send_sem=sems[3 * item].at[i],
            recv_sem=sems[3 * item + 1].at[i],
            device_id={"dp": dp, "y": y, "z": z},
            device_id_type=pl.DeviceIdType.MESH,
        )

    def local(item):
        kind = kinds[item]
        n, route, own = routes(kind, sizes, me)
        if kind in ("plane", "owners"):
            block = z
        else:
            block = own if kind.endswith("swap") else None
        src = ins[item] if block is None else ins[item].at[block]
        return pltpu.make_async_copy(src, outs[item].at[own], sems[3 * item + 2])

    for item, kind in enumerate(kinds):
        n, route, own = routes(kind, sizes, me)
        if kind == "owners":
            def send(i, carry, item=item):
                self_here = mine & (i == dp * nz + z)

                @pl.when(self_here)
                def _():
                    local(item).start()

                @pl.when(jnp.logical_not(self_here))
                def _():
                    remote(item, i).start()

                return carry

            lax.fori_loop(0, n, send, 0)
        else:
            def send(step, carry, item=item, n=n, own=own):
                remote(item, lax.rem(own + step, n)).start()
                return carry

            lax.fori_loop(1, n, send, 0)
            local(item).start()

    for item, kind in enumerate(kinds):
        n, route, own = routes(kind, sizes, me)
        if kind == "owners":
            def finish(i, carry, item=item):
                @pl.when(jnp.logical_not(mine & (i == dp * nz + z)))
                def _():
                    remote(item, i).wait_send()

                return carry

            lax.fori_loop(0, n, finish, 0)

            def collect(i, carry, item=item):
                @pl.when(jnp.logical_not(mine & (i == y * nz + z)))
                def _():
                    arrival(item, i).wait_recv()

                return carry

            lax.fori_loop(0, ny * nz, collect, 0)

            @pl.when(mine)
            def _(item=item):
                local(item).wait()
        else:
            def finish(step, carry, item=item, n=n, own=own):
                peer = lax.rem(own + step, n)
                remote(item, peer).wait_send()
                arrival(item, peer).wait_recv()
                return carry

            lax.fori_loop(1, n, finish, 0)
            local(item).wait()


def exchange(name, collective_id, sizes, *items):
    arrays = [item[0] for item in items]
    kinds = tuple(item[1] for item in items)
    ndp, ny, nz = sizes
    shapes, scratch = [], []
    for array, kind in zip(arrays, kinds):
        if kind in ("plane", "owners"):
            senders, targets = ny * nz, (ny * nz if kind == "plane" else ndp * nz)
            block = array.shape[1:]
        else:
            senders = targets = {"dp": ndp, "y": ny, "z": nz}[kind.split("_")[0]]
            block = array.shape[1:] if kind.endswith("swap") else array.shape
        shapes.append(jax.ShapeDtypeStruct((senders,) + block, array.dtype))
        scratch += [
            pltpu.SemaphoreType.DMA((targets,)),
            pltpu.SemaphoreType.DMA((senders,)),
            pltpu.SemaphoreType.DMA(()),
        ]
    return pl.pallas_call(
        functools.partial(exchange_kernel, kinds, sizes),
        out_shape=shapes,
        in_specs=[pl.BlockSpec(memory_space=pltpu.VMEM)] * len(arrays),
        out_specs=[pl.BlockSpec(memory_space=pltpu.VMEM)] * len(arrays),
        scratch_shapes=scratch,
        compiler_params=pltpu.CompilerParams(
            collective_id=collective_id, has_side_effects=True
        ),
        name=name,
    )(*arrays)


def place(dp, y, z):
    return {"dp": dp, "y": y, "z": z}


def coordinates():
    return lax.axis_index("dp"), lax.axis_index("y"), lax.axis_index("z")


def push(src, dst, send_sem, recv_sem, device):
    return pltpu.make_async_remote_copy(
        src_ref=src, dst_ref=dst, send_sem=send_sem, recv_sem=recv_sem,
        device_id=device, device_id_type=pl.DeviceIdType.MESH,
    )


def others(n, own, body):
    def step(i, carry):
        body(lax.rem(own + i, n))
        return carry

    lax.fori_loop(1, n, step, 0)


def greet_rings(sizes):
    dp, y, z = coordinates()
    ndp, ny, nz = sizes
    barrier = pltpu.get_barrier_semaphore()

    def hello(device):
        pl.semaphore_signal(barrier, inc=1, device_id=device, device_id_type=pl.DeviceIdType.MESH)

    others(nz, z, lambda j: hello(place(dp, y, j)))
    others(ny, y, lambda j: hello(place(dp, j, z)))
    others(ndp, dp, lambda j: hello(place(j, y, z)))
    pl.semaphore_wait(barrier, nz + ny + ndp - 3)


def fetch_kernel(sizes, ad, kv, packet, facts, ad_o, kv_o, packet_o, facts_o,
                 z_send, z_recv, y_send, y_recv, x_send, x_recv, mate_send, mate_recv, own_sem):
    dp, y, z = coordinates()
    ndp, ny, nz = sizes
    nx = ndp // 2
    x, core = dp // 2, lax.rem(dp, 2)
    mate = place(2 * x + 1 - core, y, z)

    keep = [
        pltpu.make_async_copy(ad.at[z], ad_o.at[dp, y, z], own_sem.at[0]),
        pltpu.make_async_copy(kv.at[z], kv_o.at[y, z], own_sem.at[1]),
        pltpu.make_async_copy(packet.at[z], packet_o.at[z], own_sem.at[2]),
        pltpu.make_async_copy(facts.at[z], facts_o.at[z], own_sem.at[3]),
    ]
    for copy in keep:
        copy.start()
    greet_rings(sizes)

    def z_copy(item, peer, slot):
        src, dst = [
            (ad.at[peer], ad_o.at[dp, y, slot]),
            (kv.at[peer], kv_o.at[y, slot]),
            (packet.at[peer], packet_o.at[slot]),
            (facts.at[peer], facts_o.at[slot]),
        ][item]
        return push(src, dst, z_send.at[item, peer], z_recv.at[item, slot], place(dp, y, peer))

    def y_copy(item, peer, slot):
        src, dst = [
            (ad_o.at[dp, y], ad_o.at[dp, slot]),
            (kv_o.at[y], kv_o.at[slot]),
        ][item]
        return push(src, dst, y_send.at[item, peer], y_recv.at[item, slot], place(dp, peer, z))

    def x_copy(peer, slot):
        return push(
            ad_o.at[dp], ad_o.at[2 * slot + core], x_send.at[peer], x_recv.at[slot],
            place(2 * peer + core, y, z),
        )

    def mate_copy(block, core_of):
        slot = 2 * block + core_of
        return push(ad_o.at[slot], ad_o.at[slot], mate_send.at[block], mate_recv.at[block], mate)

    for item in range(4):
        others(nz, z, lambda j, item=item: z_copy(item, j, z).start())
    for item in range(2):
        others(nz, z, lambda j, item=item: z_copy(item, j, j).wait_recv())
        keep[item].wait()
        others(ny, y, lambda j, item=item: y_copy(item, j, y).start())
    others(ny, y, lambda j: y_copy(0, j, j).wait_recv())
    others(nx, x, lambda j: x_copy(j, x).start())
    mate_copy(x, core).start()

    def forward(j):
        x_copy(j, j).wait_recv()
        mate_copy(j, core).start()

    others(nx, x, forward)
    for item in (2, 3):
        others(nz, z, lambda j, item=item: z_copy(item, j, j).wait_recv())
        keep[item].wait()
    others(ny, y, lambda j: y_copy(1, j, j).wait_recv())
    mate_copy(x, 1 - core).wait_recv()
    others(nx, x, lambda j: mate_copy(j, 1 - core).wait_recv())
    for item in range(4):
        others(nz, z, lambda j, item=item: z_copy(item, j, z).wait_send())
    for item in range(2):
        others(ny, y, lambda j, item=item: y_copy(item, j, y).wait_send())
    others(nx, x, lambda j: x_copy(j, x).wait_send())
    mate_copy(x, core).wait_send()
    others(nx, x, lambda j: mate_copy(j, core).wait_send())


def fetch(sizes, ad, kv, packet, facts):
    ndp, ny, nz = sizes
    shape = jax.ShapeDtypeStruct
    dma = pltpu.SemaphoreType.DMA
    vmem = pl.BlockSpec(memory_space=pltpu.VMEM)
    return pl.pallas_call(
        functools.partial(fetch_kernel, sizes),
        out_shape=[
            shape((ndp, ny) + ad.shape, ad.dtype),
            shape((ny,) + kv.shape, kv.dtype),
            shape(packet.shape, packet.dtype),
            shape(facts.shape, facts.dtype),
        ],
        in_specs=[vmem] * 4,
        out_specs=[vmem] * 4,
        scratch_shapes=[
            dma((4, nz)), dma((4, nz)), dma((2, ny)), dma((2, ny)), dma((ndp,)), dma((ndp,)),
            dma((ndp,)), dma((ndp,)), dma((4,)),
        ],
        compiler_params=pltpu.CompilerParams(collective_id=1, has_side_effects=True),
        name="fetch",
    )(ad, kv, packet, facts)


def settle_kernel(sizes, terms, out, got, total, mid, send, recv, own_sem):
    dp, y, z = coordinates()
    ndp, ny, nz = sizes
    greet_rings(sizes)

    def share_copy(peer, slot):
        return push(terms.at[peer], got.at[slot], send.at[0, peer], recv.at[0, slot], place(peer, y, z))

    def z_copy(peer, slot):
        return push(total.at[:, peer], mid.at[slot], send.at[1, peer], recv.at[1, slot], place(dp, y, peer))

    def y_copy(peer, slot):
        return push(mid.at[:, peer], out.at[dp, slot], send.at[2, peer], recv.at[2, slot], place(dp, peer, z))

    def spread_copy(peer, slot):
        return push(out.at[dp], out.at[slot], send.at[3, peer], recv.at[3, slot], place(peer, y, z))

    others(ndp, dp, lambda j: share_copy(j, dp).start())
    acc = terms[dp].astype(jnp.float32)
    others(ndp, dp, lambda j: share_copy(j, j).wait_recv())
    for step in range(1, ndp):
        acc += got[lax.rem(dp + step, ndp)].astype(jnp.float32)
    total[...] = acc.astype(total.dtype)
    others(nz, z, lambda j: z_copy(j, z).start())
    mine = pltpu.make_async_copy(total.at[:, z], mid.at[z], own_sem.at[0])
    mine.start()
    others(nz, z, lambda j: z_copy(j, j).wait_recv())
    mine.wait()
    others(ny, y, lambda j: y_copy(j, y).start())
    mine = pltpu.make_async_copy(mid.at[:, y], out.at[dp, y], own_sem.at[1])
    mine.start()
    others(ny, y, lambda j: y_copy(j, j).wait_recv())
    mine.wait()
    others(ndp, dp, lambda j: spread_copy(j, dp).start())
    others(ndp, dp, lambda j: spread_copy(j, j).wait_recv())
    others(ndp, dp, lambda j: share_copy(j, dp).wait_send())
    others(nz, z, lambda j: z_copy(j, z).wait_send())
    others(ny, y, lambda j: y_copy(j, y).wait_send())
    others(ndp, dp, lambda j: spread_copy(j, dp).wait_send())


def settle(sizes, terms):
    ndp, ny, nz = sizes
    most = max(sizes)
    block = terms.shape[3:]
    vmem = pl.BlockSpec(memory_space=pltpu.VMEM)
    return pl.pallas_call(
        functools.partial(settle_kernel, sizes),
        out_shape=jax.ShapeDtypeStruct(terms.shape, terms.dtype),
        in_specs=[vmem],
        out_specs=vmem,
        scratch_shapes=[
            pltpu.VMEM(terms.shape, terms.dtype),
            pltpu.VMEM((ny, nz) + block, terms.dtype),
            pltpu.VMEM((nz, ny) + block, terms.dtype),
            pltpu.SemaphoreType.DMA((4, most)),
            pltpu.SemaphoreType.DMA((4, most)),
            pltpu.SemaphoreType.DMA((2,)),
        ],
        compiler_params=pltpu.CompilerParams(collective_id=5, has_side_effects=True),
        name="settle",
    )(terms)


def compress(keys, values, learned):
    tokens = keys.shape[0]
    k = keys.reshape(tokens, KEY_VALUE_HEADS, HEAD_SIZE)
    v = values.reshape(tokens, KEY_VALUE_HEADS, HEAD_SIZE)
    c = learned.reshape(COMPRESSED_ROWS, KEY_VALUE_HEADS, HEAD_SIZE)
    score = jnp.einsum("cpf,ipf->pci", c, k, preferred_element_type=jnp.float32) * SOFTMAX_SCALE
    weight = jax.nn.softmax(score, axis=-1).astype(jnp.bfloat16)
    short = lambda rows: jnp.einsum(
        "wio,owx->wix", weight, rows, preferred_element_type=jnp.float32
    ).astype(jnp.bfloat16)
    return short(k), short(v)


def attend_local(queries, keys, values, offset):
    slots, tokens = queries.shape[0], keys.shape[0]
    q = queries.reshape(slots, KEY_VALUE_HEADS, GROUP, HEAD_SIZE)
    k = keys.reshape(tokens, KEY_VALUE_HEADS, HEAD_SIZE)
    v = values.reshape(tokens, KEY_VALUE_HEADS, HEAD_SIZE)
    score = jnp.einsum("shgd,nhd->hsgn", q, k, preferred_element_type=jnp.float32) * SOFTMAX_SCALE
    position = offset + jnp.arange(slots, dtype=jnp.int32)
    seen = jnp.arange(tokens, dtype=jnp.int32)[None, :] <= position[:, None]
    seen = seen[None, :, None, :]
    score = jnp.where(seen, score, NEGATIVE_FLOOR)
    peak = jnp.max(score, axis=-1)
    prob = jnp.where(seen, jnp.exp(score - peak[..., None]), 0.0)
    total = jnp.sum(prob, axis=-1)
    acc = jnp.einsum(
        "hsgn,nhd->hsgd", prob.astype(jnp.bfloat16), v, preferred_element_type=jnp.float32
    )
    out = (acc / total[..., None]).astype(jnp.bfloat16)
    return out.reshape(KEY_VALUE_HEADS, slots, GROUP * HEAD_SIZE), peak + jnp.log(total)


def shards(sizes, queries, keys, values, learned, span_len, span_offset, destination, cotangent,
           adapter_a, adapter_b):
    ndp, ny, nz = sizes
    decoders = ny * nz
    model = queries.shape[1]
    wide = model // nz
    narrow = wide // ny
    rows = nz * SLOTS
    dp, y = lax.axis_index("dp"), lax.axis_index("y")

    live = (jnp.arange(SLOTS, dtype=jnp.int32) < span_len[0, 0])[:, None]
    dy = jnp.where(live, cotangent, jnp.zeros_like(cotangent))
    ck, cv = compress(keys, values, learned)
    out_local, lse = attend_local(queries, keys, values, span_offset[0, 0])
    by_head = lambda array: array.reshape(SLOTS, nz, wide).transpose(1, 0, 2)
    packet = jnp.concatenate([by_head(queries), by_head(dy), out_local], axis=-1)
    facts = jnp.concatenate([destination.astype(jnp.float32), live.astype(jnp.float32)], axis=1)
    facts = jnp.concatenate([lse, jnp.broadcast_to(facts[None], (nz, SLOTS, 2))], axis=-1)
    facts = jnp.pad(facts, ((0, 0), (0, 0), (0, 128 - facts.shape[-1])))
    quarters = wide // 128
    chunks = jnp.stack([adapter_a[0], adapter_b[0]]).reshape(2, RANK, nz, quarters, 128)
    chunks = chunks.transpose(0, 3, 2, 1, 4).reshape(2 * quarters, nz, RANK, 128)
    share = 2 * quarters // ndp
    ad = lax.dynamic_slice_in_dim(chunks, dp * share, share, 0)
    ad = ad.transpose(1, 0, 2, 3).reshape(nz, share * RANK, 128)

    ad, short, packet, facts = fetch(
        sizes, ad, jnp.concatenate([ck, cv], axis=-1), packet, facts
    )
    ad = ad.reshape(ndp, decoders, share, RANK, 128)
    if share > 1:
        ad = ad.transpose(0, 2, 1, 3, 4)
    ad = ad.reshape(2, quarters, decoders * RANK, 128)
    downs, ups = ad[0], ad[1]
    packet = packet.reshape(rows, -1)
    facts = facts.reshape(rows, -1)
    q, dy, out_local = packet[:, :wide], packet[:, wide : 2 * wide], packet[:, 2 * wide : 3 * wide]
    short = short.reshape(ny * rows, 2 * HEAD_SIZE)
    ck, cv = short[:, :HEAD_SIZE], short[:, HEAD_SIZE:]
    lse, target, live = facts[:, :GROUP], facts[:, GROUP : GROUP + 1], facts[:, GROUP + 1 : GROUP + 2]

    heads = q.reshape(rows, GROUP, HEAD_SIZE)
    score = jnp.einsum("rgd,kd->grk", heads, ck, preferred_element_type=jnp.float32) * SOFTMAX_SCALE
    segment = y * nz + jnp.arange(rows, dtype=jnp.int32) // SLOTS
    source = jnp.arange(ny * rows, dtype=jnp.int32) // COMPRESSED_ROWS
    seen = (source[None, :] < segment[:, None])[None]
    score = jnp.where(seen, score, NEGATIVE_FLOOR)
    lse = lse.T
    peak = jnp.maximum(lse, jnp.max(score, axis=-1))
    prob = jnp.where(seen, jnp.exp(score - peak[..., None]), 0.0)
    weight = jnp.exp(lse - peak)
    total = weight + jnp.sum(prob, axis=-1)
    acc = jnp.einsum(
        "grk,kd->grd", prob.astype(jnp.bfloat16), cv, preferred_element_type=jnp.float32
    )
    home = out_local.reshape(rows, GROUP, HEAD_SIZE).transpose(1, 0, 2).astype(jnp.float32)
    attn = (acc + weight[..., None] * home) / total[..., None]
    attn = attn.transpose(1, 0, 2).reshape(rows, wide)
    attn = jnp.where(live > 0.5, attn, 0.0).astype(jnp.bfloat16)

    column = jnp.arange(decoders * RANK, dtype=jnp.int32)
    column_decoder, column_rank = column // RANK, column % RANK
    own = target.astype(jnp.int32) == column_decoder[None, :]
    pick = column_rank[:, None] == jnp.arange(RANK, dtype=jnp.int32)[None, :]
    across = (((1,), (1,)), ((), ()))

    def narrowed(left, right):
        full = sum(
            lax.dot_general(
                left[:, 128 * i : 128 * (i + 1)], right[i], across,
                preferred_element_type=jnp.float32,
            )
            for i in range(quarters)
        )
        return lax.dot_general(
            pick.astype(jnp.float32), jnp.where(own, full, 0.0), (((0,), (1,)), ((), ())),
            precision=HIGH, preferred_element_type=jnp.float32,
        )

    x = attn.astype(jnp.float32)
    square = jnp.sum(x * x, axis=1)[None]
    partial = jnp.concatenate(
        [narrowed(attn, downs), narrowed(dy, ups), square, jnp.zeros((7, rows), jnp.float32)], axis=0
    )
    slices = lambda array: array.reshape(rows, ny, narrow).transpose(1, 0, 2)
    columns = jnp.concatenate([slices(attn), slices(dy)], axis=-1)
    partial, columns = exchange("sums", 3, sizes, (partial, "z_spread"), (columns, "y_swap"))
    sums = jnp.sum(partial, axis=0)
    rs = lax.rsqrt(sums[2 * RANK : 2 * RANK + 1] / model + EPS)
    hid_exact = sums[:RANK] * rs
    hid = hid_exact.astype(jnp.bfloat16)
    back = (SCALE * sums[RANK : 2 * RANK]).astype(jnp.bfloat16)
    dot_mean = jnp.sum(back.astype(jnp.float32) * hid_exact, axis=0, keepdims=True) / model
    rs_column, mean_column = rs.T, dot_mean.T
    spread = lax.dot_general(
        back, pick.astype(jnp.bfloat16), (((0,), (1,)), ((), ())), preferred_element_type=jnp.float32
    )
    spread = jnp.where(own, spread, 0.0).astype(jnp.bfloat16)
    dn = jnp.concatenate(
        [jnp.dot(spread, downs[i], preferred_element_type=jnp.float32) for i in range(quarters)], axis=1
    )
    nrm = x * rs_column
    d_rows = (dy.astype(jnp.float32) + rs_column * (dn - nrm * mean_column)).astype(jnp.bfloat16)

    scaled = (back.astype(jnp.float32) * rs).astype(jnp.bfloat16)
    small = jnp.concatenate(
        [hid, scaled, jnp.broadcast_to(target.T, (RANK, rows)).astype(jnp.bfloat16)], axis=0
    )
    d_rows, small = exchange(
        "rows", 4, sizes, (d_rows.reshape(nz, SLOTS, wide), "z_swap"), (small, "y_spread")
    )
    grad_rows = d_rows.transpose(1, 0, 2).reshape(SLOTS, model)
    columns = columns.reshape(ny * rows, 2 * narrow)
    small = small.transpose(1, 0, 2).reshape(3 * RANK, ny * rows)
    chosen = (
        small[2 * RANK].astype(jnp.int32)[None, :]
        == jnp.arange(decoders, dtype=jnp.int32)[:, None]
    )[:, None, :]

    def gathered(values_):
        left = jnp.where(chosen, values_[None], jnp.zeros((), jnp.bfloat16))
        return jnp.dot(
            left.reshape(decoders * RANK, ny * rows), columns, preferred_element_type=jnp.float32
        )

    from_hid = SCALE * gathered(small[:RANK])
    from_back = gathered(small[RANK : 2 * RANK])
    is_a = (jnp.arange(2 * narrow, dtype=jnp.int32) < narrow)[None, :]
    terms = jnp.where(is_a, from_back, from_hid).astype(jnp.bfloat16)
    terms = terms.reshape(ny, nz, ndp, RANK // ndp, 2 * narrow).transpose(2, 0, 1, 3, 4)
    grads = settle(sizes, terms)
    final = lambda part: part.transpose(0, 3, 2, 1, 4).reshape(1, RANK, model).astype(jnp.float32)
    return grad_rows, final(grads[..., :narrow]), final(grads[..., narrow:])


def solution(mesh):
    ndp, nctx = mesh.devices.shape
    nz = KEY_VALUE_HEADS
    sizes = (ndp, nctx // nz, nz)
    fine = Mesh(mesh.devices.reshape(sizes), ("dp", "y", "z"))
    ctx = ("y", "z")
    both = ("dp", "y", "z")
    in_specs = (
        P(both, None),
        P(both, None),
        P(both, None),
        P(),
        P("dp", ctx),
        P("dp", ctx),
        P(both, None),
        P(both, None),
        P(ctx, None, None),
        P(ctx, None, None),
    )
    out_specs = (P(both, None), P(ctx, None, None), P(ctx, None, None))
    return jax.shard_map(
        functools.partial(shards, sizes), mesh=fine, in_specs=in_specs, out_specs=out_specs,
        check_vma=False,
    )
```
